128 devices in a mesh: ctx: 32 (over x, y, z_lo), head: 4 (over z_hi, core).
Axes of the slice: x: 4, y: 4, z: 4 (z_hi: 2, z_lo: 2; z = z_hi * 2 + z_lo), core: 2. Of those that a mesh axis runs over, the one named last changes fastest.
Arguments:
- tokens: bfloat16 [2, 8192, 2048], P(None, 'ctx'), may hold values from -6 to 6
- w_qkv: bfloat16 [2048, 4, 1536], P(None, 'head'), as said below
- w_rate: bfloat16 [2048, 4], P(None, 'head'), may hold values from -0.125 to 0.125
- w_out: bfloat16 [4, 512, 2048], P('head'), may hold values from -0.125 to 0.125
- fw_gain: float32 [4, 512], P('head'), may hold values from 0.25 to 1.75
- fast_first: float32 [4, 512, 512], P('head'), may hold values from -0.25 to 0.25
- fast_third: float32 [4, 512, 512], P('head'), may hold values from -0.25 to 0.25
- fast_second: float32 [4, 512, 512], P('head'), may hold values from -0.25 to 0.25
Outputs:
- mixed: bfloat16 [2, 8192, 2048], P(None, 'ctx', 'head')
- new_first: float32 [4, 512, 512], P('head')
- new_third: float32 [4, 512, 512], P('head')
- new_second: float32 [4, 512, 512], P('head')
The draws below stay inside these ranges and needn't reach their ends.
Inputs may be any that keep to these rules, and one draw needn't show every extreme that they name: `w_qkv`: A projection scaled by its fan-in 2048.
All inputs are finite; a program needn't handle non-finite values.
Results may differ from the reference program's by a relative error of at most 0.039.
Values may be sent and summed in bfloat16 or wider, within the bound.
No kernel may reach another device: no remote copies, remote signals or barrier semaphores. Data moves between devices by JAX's collectives and lax.ppermute only.
A program may use at most 128 MiB of HBM per device.

```python
import jax
import jax.numpy as jnp
from jax import lax

D = 2048
HEADS = 4
DH = 512
FH = 512
TOK_DEV = 256
WINDOW = 2048
BLOCKS = 2
NS_STEPS = 5
BLOCK = 8192


def draw_tokens(key, part):
    base = jax.random.normal(jax.random.fold_in(key, 11), (BLOCKS, BLOCK, D), jnp.float32)
    base = jnp.clip(base, -6.0, 6.0)
    return base.astype(jnp.bfloat16)


def draw_w_qkv(key, part):
    base = jax.random.normal(jax.random.fold_in(key, 23), (D, HEADS, 3 * DH), jnp.float32)
    base = jnp.clip(base, -6.0, 6.0) * D ** (-0.5)
    return base.astype(jnp.bfloat16)


def level_of(key, shape, pieces, low, high):
    loudness, own = 1.0, jax.random.fold_in(key, 6)
    for axis_at, parts in pieces:
        steps = jnp.exp(jax.random.uniform(jax.random.fold_in(own, axis_at), (parts,), jnp.float32, low / len(pieces), high / len(pieces)))
        loudness = loudness * jnp.repeat(steps, shape[axis_at] // parts).reshape([-1 if axis == axis_at else 1 for axis in range(len(shape))])
    return loudness


def scatter_about(rng, shape, spread, bound, cuts=(), held_as=jnp.bfloat16):
    drawn = spread * jax.random.normal(rng, shape, jnp.float32)
    if cuts:
        drawn = drawn * level_of(rng, shape, cuts, -0.22, 0.18)
    return jnp.clip(drawn, -bound, bound).astype(held_as)


def setup_inputs(seed: int = 0) -> dict:
    key_list = jax.random.split(jax.random.key(seed), 9)
    tokens = draw_tokens(jax.random.fold_in(key_list[8], 71), 0)
    w_qkv = draw_w_qkv(jax.random.fold_in(key_list[8], 71), 0)
    w_rate = scatter_about(key_list[2], (D, HEADS), D ** -0.5, 0.125, ((1, 4),))
    w_out = scatter_about(key_list[3], (HEADS, DH, D), D ** -0.5, 0.125, ((0, 4),))
    fw_gain = jnp.clip(1.0 + 0.15 * jax.random.normal(key_list[4], (HEADS, DH), jnp.float32), 0.25, 1.75)
    fast_first = scatter_about(key_list[5], (HEADS, DH, FH), DH ** -0.5, 0.25, ((0, 4),), jnp.float32)
    fast_third = scatter_about(key_list[6], (HEADS, DH, FH), DH ** -0.5, 0.25, ((0, 4),), jnp.float32)
    fast_second = scatter_about(key_list[7], (HEADS, FH, DH), FH ** -0.5, 0.25, ((0, 4),), jnp.float32)
    return dict(tokens=tokens, w_qkv=w_qkv, w_rate=w_rate, w_out=w_out, fw_gain=fw_gain, fast_first=fast_first, fast_third=fast_third, fast_second=fast_second)


coeff_a = 3.4445
coeff_b = -4.775
coeff_c = 2.0315
fast_step = 0.5
norm_eps = 1e-06

def inner_rows(left, right):
    return lax.dot_general(left, right, (((0,), (0,)), ((), ())), preferred_element_type=jnp.float32)

def silu_grad(hidden):
    sigma = jax.nn.sigmoid(hidden)
    return sigma * (1.0 + hidden * (1.0 - sigma))

def narrow(weights):
    return tuple((weight.astype(jnp.bfloat16) for weight in weights))

def fast_apply(queries, narrowed):
    hidden_one = jnp.dot(queries, narrowed[0], preferred_element_type=jnp.float32)
    hidden_three = jnp.dot(queries, narrowed[1], preferred_element_type=jnp.float32)
    activ = (jax.nn.silu(hidden_one) * hidden_three).astype(jnp.bfloat16)
    return jnp.dot(activ, narrowed[2], preferred_element_type=jnp.float32)

def fast_grads(keys, values, rates, narrowed):
    hidden_one = jnp.dot(keys, narrowed[0], preferred_element_type=jnp.float32)
    hidden_three = jnp.dot(keys, narrowed[1], preferred_element_type=jnp.float32)
    activ = (jax.nn.silu(hidden_one) * hidden_three).astype(jnp.bfloat16)
    target = (-rates[:, None] * values.astype(jnp.float32)).astype(jnp.bfloat16)
    grad_second = inner_rows(activ, target)
    dactiv = lax.dot_general(target, narrowed[2], (((1,), (1,)), ((), ())), preferred_element_type=jnp.float32)
    d_first = (dactiv * hidden_three * silu_grad(hidden_one)).astype(jnp.bfloat16)
    d_third = (dactiv * jax.nn.silu(hidden_one)).astype(jnp.bfloat16)
    return (inner_rows(keys, d_first), inner_rows(keys, d_third), grad_second)

def gram_of(current):
    return lax.dot_general(current, current, (((0,), (0,)), ((), ())), precision=lax.Precision.HIGHEST, preferred_element_type=jnp.float32)

def ns_update(current, gram):
    poly = coeff_b * gram + coeff_c * jnp.dot(gram, gram, precision=lax.Precision.HIGHEST)
    return coeff_a * current + jnp.dot(current, poly, precision=lax.Precision.HIGHEST)

def orthogonalize(grad):
    current = grad / jnp.sqrt(jnp.sum(grad * grad) + norm_eps)
    for step_num in range(NS_STEPS):
        current = ns_update(current, gram_of(current))
    return current

def window_softmax(query_rows, key_rows, value_rows, first_key):
    row_count = query_rows.shape[0]
    key_span = key_rows.shape[0]
    window_len = key_span - row_count
    scores = lax.dot_general(query_rows, key_rows, (((1,), (1,)), ((), ())), preferred_element_type=jnp.float32)
    scores = scores * query_rows.shape[1] ** (-0.5)
    offsets = window_len + lax.broadcasted_iota(jnp.int32, (row_count, key_span), 0) - lax.broadcasted_iota(jnp.int32, (row_count, key_span), 1)
    positions = first_key + lax.broadcasted_iota(jnp.int32, (row_count, key_span), 1)
    allowed = (offsets >= 0) & (offsets < window_len) & (positions >= 0)
    scores = jnp.where(allowed, scores, -1e+30)
    highest = lax.optimization_barrier(jnp.max(scores, axis=1, keepdims=True))
    weights = jnp.exp(scores - highest)
    weights = (weights / lax.optimization_barrier(jnp.sum(weights, axis=1, keepdims=True))).astype(jnp.bfloat16)
    return jnp.dot(weights, value_rows, preferred_element_type=jnp.float32)

def attend(queries, keys, values):
    total_rows = queries.shape[0]
    pad_keys = jnp.pad(keys, ((WINDOW, 0), (0, 0)))
    pad_values = jnp.pad(values, ((WINDOW, 0), (0, 0)))

    def one_block(block_num):
        start = (block_num * TOK_DEV).astype(jnp.int32)
        query_rows = lax.dynamic_slice_in_dim(queries, start, TOK_DEV, 0)
        key_rows = lax.dynamic_slice_in_dim(pad_keys, start, WINDOW + TOK_DEV, 0)
        value_rows = lax.dynamic_slice_in_dim(pad_values, start, WINDOW + TOK_DEV, 0)
        return window_softmax(query_rows, key_rows, value_rows, start - WINDOW)
    outputs = lax.map(one_block, jnp.arange(total_rows // TOK_DEV, dtype=jnp.int32))
    return outputs.reshape(total_rows, DH)

def reference(tokens, w_qkv, w_rate, w_out, fw_gain, fast_first, fast_third, fast_second):
    flat = tokens.reshape(BLOCKS * BLOCK, D)
    projected = jnp.dot(flat, w_qkv.reshape(D, HEADS * 3 * DH), preferred_element_type=jnp.float32).astype(jnp.bfloat16)
    projected = projected.reshape(BLOCKS * BLOCK, HEADS, 3, DH)
    rates = jax.nn.softplus(jnp.dot(flat, w_rate, preferred_element_type=jnp.float32))
    mixed = jnp.zeros((BLOCKS * BLOCK, D), jnp.float32)
    final_first = []
    final_third = []
    final_second = []
    for head_num in range(HEADS):
        queries = projected[:, head_num, 0]
        keys = projected[:, head_num, 1]
        values = projected[:, head_num, 2]
        attended = attend(queries, keys, values)
        current = (fast_first[head_num], fast_third[head_num], fast_second[head_num])
        outputs = []
        for block_num in range(BLOCKS):
            lower = block_num * BLOCK
            upper = lower + BLOCK
            outputs.append(fast_apply(queries[lower:upper], narrow(current)))
            if block_num + 1 < BLOCKS:
                grads = fast_grads(keys[lower:upper], values[lower:upper], rates[lower:upper, head_num], narrow(current))
                current = tuple((weight - fast_step * orthogonalize(grad) for weight, grad in zip(current, grads)))
        fast_out = jnp.concatenate(outputs, axis=0)
        normed = fast_out * lax.rsqrt(lax.optimization_barrier(jnp.mean(fast_out * fast_out, axis=1, keepdims=True)) + norm_eps) * fw_gain[head_num]
        combined = (attended + normed).astype(jnp.bfloat16)
        mixed = mixed + jnp.dot(combined, w_out[head_num], preferred_element_type=jnp.float32)
        final_first.append(current[0])
        final_third.append(current[1])
        final_second.append(current[2])
    mixed = mixed.astype(jnp.bfloat16).reshape(BLOCKS, BLOCK, D)
    return (mixed, jnp.stack(final_first), jnp.stack(final_third), jnp.stack(final_second))
```

```python
import jax
import jax.numpy as jnp
from jax import lax
from jax.experimental import pallas as pl
from jax.experimental.pallas import tpu as pltpu
from jax.sharding import PartitionSpec as P

NS_STEPS = 5
HALF = 256
SUPER = 512
REACH = 4
BF = jnp.bfloat16
F32 = jnp.float32

coeff_a = 3.4445
coeff_b = -4.775
coeff_c = 2.0315
fast_step = 0.5
norm_eps = 1e-06
MASKED = -1e30

CTX_X, CTX_Y, CTX_Z = 4, 4, 2


def nn(left, right):
    return lax.dot_general(left, right, (((1,), (0,)), ((), ())), preferred_element_type=F32)


def nt(left, right):
    return lax.dot_general(left, right, (((1,), (1,)), ((), ())), preferred_element_type=F32)


def tn(left, right):
    return lax.dot_general(left, right, (((0,), (0,)), ((), ())), preferred_element_type=F32)


def moved(value, route):
    pairs = []
    for ctx in range(CTX_X * CTX_Y * CTX_Z):
        x, y, z = ctx // 8, (ctx // 2) % 4, ctx % 2
        for head in range(4):
            target = route(x, y, z, head // 2, head % 2)
            if target is not None:
                tx, ty, tz, th, tc = target
                pairs.append((ctx * 4 + head, (tx * 8 + ty * 2 + tz) * 4 + th * 2 + tc))
    return lax.ppermute(value, ("ctx", "head"), pairs)


def to_role_same(x, y, z, zh, core):
    return (x, (y & 2) + core, z, zh, y & 1)


def to_role_other(x, y, z, zh, core):
    return (x, (y & 2) + core, 1 - z, zh, y & 1)


def quads_on(steps):
    def route(x, y, z, zh, core):
        place = z * 8 + 2 * x + (y >> 1) + steps
        if place >= 16:
            return None
        quad = place % 8
        return (quad // 2, (quad % 2) * 2 + (y & 1), place // 8, zh, core)

    return route


def across(x, y, z, zh, core):
    return (x, y ^ 2, z, zh, core)


def other_core(x, y, z, zh, core):
    return (x, y, z, zh, 1 - core)


def other_pair(x, y, z, zh, core):
    return (x, y, z, 1 - zh, core)


def vmem():
    return pl.BlockSpec(memory_space=pltpu.VMEM)


def smem():
    return pl.BlockSpec(memory_space=pltpu.SMEM)


def call(kernel, specs, outs, flops=1 << 20, scratch=(), limit=16):
    return pl.pallas_call(
        kernel,
        in_specs=specs,
        out_specs=[vmem()] * len(outs),
        out_shape=[jax.ShapeDtypeStruct(shape, dtype) for shape, dtype in outs],
        scratch_shapes=list(scratch),
        compiler_params=pltpu.CompilerParams(vmem_limit_bytes=limit << 20),
        cost_estimate=pl.CostEstimate(flops=flops, bytes_accessed=1 << 10, transcendentals=0),
        name=kernel.__name__,
    )


CHUNK = 256
CHUNKS = 6


def project(place, tokens_ref, w_ref, natural_ref, same, other):
    z = place[0]
    tokens = tokens_ref[...].reshape(2 * HALF, -1)
    for j in (2, 3, 0, 1, 4, 5):
        columns = slice(j * CHUNK, (j + 1) * CHUNK)
        result = nn(tokens, w_ref[:, columns]).astype(BF)
        low, high = result[:HALF], result[HALF:]
        natural_ref[0, :, columns] = low
        natural_ref[1, :, columns] = high
        part = slice((j % 2) * CHUNK, (j % 2 + 1) * CHUNK)
        rows = slice(j // 2 * HALF, (j // 2 + 1) * HALF)
        same[rows, part] = jnp.where(z == 0, low, high)
        other[rows, part] = jnp.where(z == 0, high, low)


def run_project(place, tokens, weights):
    return call(
        project,
        [smem(), vmem(), vmem()],
        [((2, HALF, 1536), BF)] + [((3 * HALF, 512), BF)] * 2,
    )(place, tokens, weights)


def spread(whole, outs, at):
    rows = outs[0].shape[0]
    for step, ref in enumerate(outs):
        start = pl.multiple_of((at ^ step) * rows, rows)
        ref[...] = whole[pl.ds(start, rows)]


def fast_grads(place, tokens_ref, rate_ref, qkv_ref, first_ref, third_ref, second_ref, *rest):
    out_ref = rest[4]
    drive = jnp.sum(
        tokens_ref[0].astype(F32) * rate_ref[...].astype(F32), axis=1, keepdims=True
    )
    rates = jnp.maximum(drive, 0.0) + jnp.log1p(jnp.exp(-jnp.abs(drive)))
    keys = qkv_ref[0, :, 512:1024]
    values = qkv_ref[0, :, 1024:]
    hidden_one = nn(keys, first_ref[...].astype(BF))
    hidden_three = nn(keys, third_ref[...].astype(BF))
    target = (-rates * values.astype(F32)).astype(BF)
    dactiv = nt(target, second_ref[...].astype(BF))
    sigma = jax.nn.sigmoid(hidden_one)
    silu = hidden_one * sigma
    activ = (silu * hidden_three).astype(BF)
    d_first = (dactiv * hidden_three * (sigma * (1.0 + hidden_one * (1.0 - sigma)))).astype(BF)
    d_third = (dactiv * silu).astype(BF)
    out_ref[0:512] = tn(keys, d_first).astype(BF)
    out_ref[512:1024] = tn(keys, d_third).astype(BF)
    out_ref[1024:1536] = tn(activ, target).astype(BF)
    spread(out_ref, rest[:4], place[4])


def summed(refs):
    total = refs[0][...].astype(F32)
    for ref in refs[1:]:
        total = total + ref[...].astype(F32)
    return total.astype(BF)


def reduce_x(place, *refs):
    refs[8][...] = summed(refs[:4])
    spread(refs[8], refs[4:8], place[5])


def reduce_y(*refs):
    refs[4][...] = summed(refs[:4])


def reduce_z(*refs):
    refs[2][...] = summed(refs[:2])


def applied(queries, first, third, second, gain):
    hidden_one = nn(queries, first)
    hidden_three = nn(queries, third)
    activ = (jax.nn.silu(hidden_one) * hidden_three).astype(BF)
    fast_out = nn(activ, second)
    mean = jnp.mean(fast_out * fast_out, axis=1, keepdims=True)
    return fast_out * lax.rsqrt(mean + norm_eps) * gain


def fast_apply(qkv_ref, first_ref, third_ref, second_ref, gain_ref, out_ref):
    out_ref[...] = applied(
        qkv_ref[0, :, :512],
        first_ref[...].astype(BF),
        third_ref[...].astype(BF),
        second_ref[...].astype(BF),
        gain_ref[...],
    )


def fast_update(
    place,
    part_zero,
    part_one,
    part_two,
    part_three,
    first_ref,
    third_ref,
    second_ref,
    qkv_ref,
    gain_ref,
    new_first_ref,
    new_third_ref,
    new_second_ref,
    normed_ref,
    current,
    grad_ref,
):
    x, y = place[4], place[5]
    for step, part in enumerate((part_zero, part_one, part_two, part_three)):
        for across_y in range(4):
            start = (x ^ step) * 384 + (y ^ across_y) * 96
            at = across_y * 96
            grad_ref[pl.ds(pl.multiple_of(start, 96), 96)] = part[at : at + 96]
    for which in range(3):
        grad = grad_ref[which * 512 : (which + 1) * 512].astype(F32)
        scale = lax.rsqrt(jnp.sum(grad * grad, keepdims=True) + norm_eps)
        current[which] = (grad * scale).astype(BF)

    def advanced():
        now = [current[which] for which in range(3)]
        grams = [nt(x, x) for x in now]
        narrow = [gram.astype(BF) for gram in grams]
        polys = [
            (coeff_b * gram + coeff_c * nn(low, low)).astype(BF)
            for gram, low in zip(grams, narrow)
        ]
        return [coeff_a * x.astype(F32) + nn(poly, x) for x, poly in zip(now, polys)]

    @pl.loop(0, NS_STEPS - 1)
    def _(step):
        for which, value in enumerate(advanced()):
            current[which] = value.astype(BF)

    last = advanced()
    old = (first_ref, third_ref, second_ref)
    new = [ref[...] - fast_step * value for ref, value in zip(old, last)]
    for ref, value in zip((new_first_ref, new_third_ref, new_second_ref), new):
        ref[...] = value
    narrow = [weight.astype(BF) for weight in new]
    normed_ref[...] = applied(qkv_ref[1, :, :512], *narrow, gain_ref[...])


ROWS = 128


def scores(place, queries_ref, own, swap_one, one, swap_two, two, out_ref, sum_ref, held):
    z, index, core = place[0], place[1], place[2]
    for tile in range(SUPER // ROWS):
        queries = queries_ref[tile * ROWS : (tile + 1) * ROWS]
        query_at = (
            ((tile // 2) ^ z) * HALF
            + (tile % 2) * ROWS
            + lax.broadcasted_iota(jnp.int32, (ROWS, SUPER), 0)
        )
        column = lax.broadcasted_iota(jnp.int32, (ROWS, SUPER), 1)
        highest = jnp.full((ROWS, 1), MASKED, F32)
        order = ((own, 0), (one, 2), (two, REACH), (swap_one, 1 + 2 * core), (swap_two, 3 - 2 * core))
        for slot, (piece, distance) in enumerate(order):
            source = z * 16 + index - distance
            part = nt(queries, piece[...]) * (512 ** (-0.5))
            if slot == 0:
                shift = z * HALF
                key_at = jnp.where(column < HALF, column + shift, column - shift)
                part = jnp.where(key_at <= query_at, part, MASKED)
            elif slot == 2:
                shift = jnp.where(source >= 16, HALF, 0)
                key_at = jnp.where(column < HALF, column + shift, column - shift)
                part = jnp.where((key_at > query_at) & (source >= 0), part, MASKED)
            else:
                part = jnp.where(source >= 0, part, MASKED)
            held[slot] = part
            highest = jnp.maximum(highest, jnp.max(part, axis=1, keepdims=True))
        total = jnp.zeros((ROWS, 1), F32)
        rows = slice(tile * ROWS, (tile + 1) * ROWS)
        for slot in range(5):
            weights = jnp.exp(held[slot] - highest)
            total = total + jnp.sum(weights, axis=1, keepdims=True)
            out_ref[slot, rows] = weights.astype(BF)
        sum_ref[rows] = jnp.broadcast_to(1.0 / total, (ROWS, 128))


def gathered(weights_ref, sum_ref, own, swap_one, one, swap_two, two, same_ref, other_ref):
    for half, out_ref in enumerate((same_ref, other_ref)):
        rows = slice(half * HALF, (half + 1) * HALF)
        result = jnp.zeros((HALF, 512), F32)
        for slot, piece in enumerate((own, one, two, swap_one, swap_two)):
            result = result + nn(weights_ref[slot, rows], piece[...])
        out_ref[...] = (result * sum_ref[rows, 0:1]).astype(BF)


def mix(place, near_ref, far_ref, normed_ref, w_ref, keep_ref, send_ref, *, block_num):
    z, core, pair = place[0], place[2], place[3]
    attended = jnp.where(z == block_num, near_ref[...], far_ref[...])
    combined = (attended.astype(F32) + normed_ref[...]).astype(BF)
    for step in range(2):
        for out_ref, whose in ((keep_ref, core), (send_ref, 1 - core)):
            column = pl.multiple_of(((pair ^ step) * 2 + whose) * 512, 512)
            out_ref[step] = nn(combined, w_ref[:, pl.ds(column, 512)]).astype(BF)


def mix_zero(*refs):
    mix(*refs, block_num=0)


def mix_one(*refs):
    mix(*refs, block_num=1)


def over_heads(place, near, far, normed, w_out, kernel):
    keep, send = call(
        kernel,
        [smem()] + [vmem()] * 4,
        [((2, HALF, 512), BF)] * 2,
    )(place, near, far, normed, w_out)
    return keep.astype(F32) + moved(send, other_core).astype(F32)


def ordered(values, *before):
    kept = lax.optimization_barrier((tuple(values), before))
    return list(kept[0])


def exchanged(pieces, axis):
    received = [pieces[0]]
    for step in range(1, len(pieces)):
        dx, dy, dz = (step if axis == name else 0 for name in "xyz")

        def route(x, y, z, zh, core):
            return (x ^ dx, y ^ dy, z ^ dz, zh, core)

        received.append(moved(pieces[step], route))
    return received


def to_pair(near):
    return near[0] + moved(near[1].astype(BF), other_pair).astype(F32)


def shards(tokens, w_qkv, w_rate, w_out, fw_gain, fast_first, fast_third, fast_second):
    width = tokens.shape[2]
    ctx, head = lax.axis_index("ctx"), lax.axis_index("head")
    x, y, z = ctx // 8, (ctx // 2) % 4, ctx % 2
    zh, core = head // 2, head % 2
    index = 4 * x + (y & 2) + core
    place = jnp.stack([z, index, core, zh, x, y]).astype(jnp.int32)
    first, third, second = fast_first[0], fast_third[0], fast_second[0]

    natural, same, other = run_project(
        place, tokens, w_qkv.reshape(width, 1536)
    )
    same = moved(same, to_role_same)
    other = moved(other, to_role_other)
    grads = call(
        fast_grads,
        [smem()] + [vmem()] * 6,
        [((384, 512), BF)] * 4,
        scratch=(pltpu.VMEM((1536, 512), BF),),
        limit=24,
    )(place, tokens, w_rate.reshape(1, width), natural, first, third, second)
    same, other = ordered([same, other], *grads)
    grads = exchanged(grads, "x")
    queries, own_keys, own_values = (
        jnp.concatenate([half[at * HALF : (at + 1) * HALF] for half in (same, other)], axis=0)
        for at in range(3)
    )
    grads = call(
        reduce_x,
        [smem()] + [vmem()] * 4,
        [((96, 512), BF)] * 4,
        scratch=(pltpu.VMEM((384, 512), BF),),
    )(place, *grads)
    (own_keys,) = ordered([own_keys], grads[0])
    two_keys = moved(own_keys, quads_on(2))
    grads = exchanged(grads, "y")
    (piece,) = call(reduce_y, [vmem()] * 4, [((96, 512), BF)])(*grads)
    (own_values,) = ordered([own_values], piece)
    two_values = moved(own_values, quads_on(2))
    (piece,) = call(reduce_z, [vmem()] * 2, [((96, 512), BF)])(*exchanged([piece] * 2, "z"))

    def onward(own, two):
        return jnp.where(y >= 2, two, own), jnp.where(core == 0, own, two)

    (two_keys,) = ordered([two_keys], piece)
    one_keys, swap_two_keys = onward(own_keys, two_keys)
    piece = exchanged([piece] * 4, "y")
    piece = jnp.concatenate(ordered(piece, one_keys), axis=0)
    one_keys = moved(one_keys, across)
    swap_two_keys = moved(swap_two_keys, other_core)
    parts = exchanged([piece] * 4, "x")
    (two_values,) = ordered([two_values], piece)
    one_values, swap_two_values = onward(own_values, two_values)
    (queries,) = ordered([queries], one_values)
    one_values = moved(one_values, across)
    swap_two_values = moved(swap_two_values, other_core)

    swap_one_keys = moved(one_keys, other_core)
    weights, sums = call(
        scores,
        [smem()] + [vmem()] * 6,
        [((5, SUPER, SUPER), BF), ((SUPER, 128), F32)],
        scratch=(pltpu.VMEM((5, ROWS, SUPER), F32),),
    )(place, queries, own_keys, swap_one_keys, one_keys, swap_two_keys, two_keys)
    swap_one_values = moved(one_values, other_core)
    near, far = call(gathered, [vmem()] * 7, [((HALF, 512), BF)] * 2)(
        weights, sums, own_values, swap_one_values, one_values, swap_two_values, two_values
    )
    parts = ordered(parts, near, far)
    near = moved(near, to_role_same)
    far = moved(far, to_role_other)

    (normed_zero,) = call(
        fast_apply, [vmem()] * 5, [((HALF, 512), F32)]
    )(natural, first, third, second, fw_gain)
    new_first, new_third, new_second, normed_one = call(
        fast_update,
        [smem()] + [vmem()] * 9,
        [((512, 512), F32)] * 3 + [((HALF, 512), F32)],
        scratch=(pltpu.VMEM((3, 512, 512), BF), pltpu.VMEM((1536, 512), BF)),
        limit=24,
    )(place, *parts, first, third, second, natural, fw_gain)
    (normed_zero,) = ordered([normed_zero], normed_one)
    half_zero = over_heads(place, near, far, normed_zero, w_out[0], mix_zero)
    half_one = over_heads(place, near, far, normed_one, w_out[0], mix_one)
    mixed = jnp.stack([to_pair(half_zero), to_pair(half_one)]).astype(BF)
    return (mixed, new_first[None], new_third[None], new_second[None])


def solution(mesh):
    placed = (
        P(None, "ctx", None),
        P(None, "head", None),
        P(None, "head"),
        P("head", None, None),
        P("head", None),
        P("head", None, None),
        P("head", None, None),
        P("head", None, None),
    )
    return jax.shard_map(
        shards,
        mesh=mesh,
        in_specs=placed,
        out_specs=(
            P(None, "ctx", "head"),
            P("head", None, None),
            P("head", None, None),
            P("head", None, None),
        ),
        check_vma=False,
    )
```

```python
import jax
import jax.numpy as jnp
from jax import lax
from jax.experimental import pallas as pl
from jax.experimental.pallas import tpu as pltpu
from jax.sharding import PartitionSpec as P

NS_STEPS = 5
FIRST_STEPS = 1
MIDDLE_STEPS = 1
HALF = 256
SUPER = 512
REACH = 4
BF = jnp.bfloat16
F32 = jnp.float32

coeff_a = 3.4445
coeff_b = -4.775
coeff_c = 2.0315
fast_step = 0.5
norm_eps = 1e-06
MASKED = -1e30

CTX_X, CTX_Y, CTX_Z = 4, 4, 2


def nn(left, right):
    return lax.dot_general(left, right, (((1,), (0,)), ((), ())), preferred_element_type=F32)


def nt(left, right):
    return lax.dot_general(left, right, (((1,), (1,)), ((), ())), preferred_element_type=F32)


def tn(left, right):
    return lax.dot_general(left, right, (((0,), (0,)), ((), ())), preferred_element_type=F32)


def moved(value, route):
    pairs = []
    for ctx in range(CTX_X * CTX_Y * CTX_Z):
        x, y, z = ctx // 8, (ctx // 2) % 4, ctx % 2
        for head in range(4):
            target = route(x, y, z, head // 2, head % 2)
            if target is not None:
                tx, ty, tz, th, tc = target
                pairs.append((ctx * 4 + head, (tx * 8 + ty * 2 + tz) * 4 + th * 2 + tc))
    return lax.ppermute(value, ("ctx", "head"), pairs)


def to_role_same(x, y, z, zh, core):
    return (x, (y & 2) + core, z, zh, y & 1)


def to_role_other(x, y, z, zh, core):
    return (x, (y & 2) + core, 1 - z, zh, y & 1)


def quads_on(steps):
    def route(x, y, z, zh, core):
        place = z * 8 + 2 * x + (y >> 1) + steps
        if place >= 16:
            return None
        quad = place % 8
        return (quad // 2, (quad % 2) * 2 + (y & 1), place // 8, zh, core)

    return route


def across(x, y, z, zh, core):
    return (x, y ^ 2, z, zh, core)


def other_core(x, y, z, zh, core):
    return (x, y, z, zh, 1 - core)


def other_pair(x, y, z, zh, core):
    return (x, y, z, 1 - zh, core)


def vmem():
    return pl.BlockSpec(memory_space=pltpu.VMEM)


def smem():
    return pl.BlockSpec(memory_space=pltpu.SMEM)


def call(kernel, specs, outs, flops=1 << 20, scratch=(), limit=16):
    return pl.pallas_call(
        kernel,
        in_specs=specs,
        out_specs=[vmem()] * len(outs),
        out_shape=[jax.ShapeDtypeStruct(shape, dtype) for shape, dtype in outs],
        scratch_shapes=list(scratch),
        compiler_params=pltpu.CompilerParams(vmem_limit_bytes=limit << 20),
        cost_estimate=pl.CostEstimate(flops=flops, bytes_accessed=1 << 10, transcendentals=0),
        name=kernel.__name__,
    )


CHUNK = 256
CHUNKS = 6


def project(place, tokens_ref, w_ref, natural_ref, same, other):
    z = place[0]
    tokens = tokens_ref[...].reshape(2 * HALF, -1)
    for j in (2, 3, 0, 1, 4, 5):
        columns = slice(j * CHUNK, (j + 1) * CHUNK)
        result = nn(tokens, w_ref[:, columns]).astype(BF)
        low, high = result[:HALF], result[HALF:]
        natural_ref[0, :, columns] = low
        natural_ref[1, :, columns] = high
        part = slice((j % 2) * CHUNK, (j % 2 + 1) * CHUNK)
        rows = slice(j // 2 * HALF, (j // 2 + 1) * HALF)
        same[rows, part] = jnp.where(z == 0, low, high)
        other[rows, part] = jnp.where(z == 0, high, low)


def run_project(place, tokens, weights):
    return call(
        project,
        [smem(), vmem(), vmem()],
        [((2, HALF, 1536), BF)] + [((3 * HALF, 512), BF)] * 2,
    )(place, tokens, weights)


def spread(whole, outs, at):
    rows = outs[0].shape[0]
    for step, ref in enumerate(outs):
        start = pl.multiple_of((at ^ step) * rows, rows)
        ref[...] = whole[pl.ds(start, rows)]


def fast_grads(place, tokens_ref, rate_ref, qkv_ref, first_ref, third_ref, second_ref, *rest):
    out_ref = rest[4]
    drive = jnp.sum(
        tokens_ref[0].astype(F32) * rate_ref[...].astype(F32), axis=1, keepdims=True
    )
    rates = jnp.maximum(drive, 0.0) + jnp.log1p(jnp.exp(-jnp.abs(drive)))
    keys = qkv_ref[0, :, 512:1024]
    values = qkv_ref[0, :, 1024:]
    hidden_one = nn(keys, first_ref[...].astype(BF))
    hidden_three = nn(keys, third_ref[...].astype(BF))
    target = (-rates * values.astype(F32)).astype(BF)
    dactiv = nt(target, second_ref[...].astype(BF))
    sigma = jax.nn.sigmoid(hidden_one)
    silu = hidden_one * sigma
    activ = (silu * hidden_three).astype(BF)
    d_first = (dactiv * hidden_three * (sigma * (1.0 + hidden_one * (1.0 - sigma)))).astype(BF)
    d_third = (dactiv * silu).astype(BF)
    out_ref[0:512] = tn(keys, d_first).astype(BF)
    out_ref[512:1024] = tn(keys, d_third).astype(BF)
    out_ref[1024:1536] = tn(activ, target).astype(BF)
    spread(out_ref, rest[:4], place[4])


def summed(refs):
    total = refs[0][...].astype(F32)
    for ref in refs[1:]:
        total = total + ref[...].astype(F32)
    return total.astype(BF)


def reduce_x(place, *refs):
    refs[8][...] = summed(refs[:4])
    spread(refs[8], refs[4:8], place[5])


def reduce_y(*refs):
    refs[4][...] = summed(refs[:4])


def reduce_z(*refs):
    refs[2][...] = summed(refs[:2])


def applied(queries, first, third, second, gain):
    hidden_one = nn(queries, first)
    hidden_three = nn(queries, third)
    activ = (jax.nn.silu(hidden_one) * hidden_three).astype(BF)
    fast_out = nn(activ, second)
    mean = jnp.mean(fast_out * fast_out, axis=1, keepdims=True)
    return fast_out * lax.rsqrt(mean + norm_eps) * gain


def fast_apply(qkv_ref, first_ref, third_ref, second_ref, gain_ref, out_ref):
    out_ref[...] = applied(
        qkv_ref[0, :, :512],
        first_ref[...].astype(BF),
        third_ref[...].astype(BF),
        second_ref[...].astype(BF),
        gain_ref[...],
    )


def advanced(now):
    grams = [nt(x, x) for x in now]
    narrow = [gram.astype(BF) for gram in grams]
    polys = [
        (coeff_b * gram + coeff_c * nn(low, low)).astype(BF)
        for gram, low in zip(grams, narrow)
    ]
    return [coeff_a * x.astype(F32) + nn(poly, x) for x, poly in zip(now, polys)]


def repeated(ref, steps):
    @pl.loop(0, steps)
    def _(step):
        for which, value in enumerate(advanced([ref[which] for which in range(3)])):
            ref[which] = value.astype(BF)


def update_start(place, parts_ref, out_ref, grad_ref):
    y = place[5]
    for at_x in range(4):
        for across_y in range(4):
            start = at_x * 384 + (y ^ across_y) * 96
            at = across_y * 96
            grad_ref[pl.ds(pl.multiple_of(start, 96), 96)] = parts_ref[
                at_x, at : at + 96
            ]
    for which in range(3):
        grad = grad_ref[which * 512 : (which + 1) * 512].astype(F32)
        scale = lax.rsqrt(jnp.sum(grad * grad, keepdims=True) + norm_eps)
        out_ref[which] = (grad * scale).astype(BF)
    repeated(out_ref, FIRST_STEPS)


def update_middle(in_ref, out_ref):
    out_ref[...] = in_ref[...]
    repeated(out_ref, MIDDLE_STEPS)


def update_end(
    in_ref,
    first_ref,
    third_ref,
    second_ref,
    qkv_ref,
    gain_ref,
    new_first_ref,
    new_third_ref,
    new_second_ref,
    normed_ref,
    held,
):
    held[...] = in_ref[...]
    repeated(held, NS_STEPS - 1 - FIRST_STEPS - MIDDLE_STEPS)
    last = advanced([held[which] for which in range(3)])
    old = (first_ref, third_ref, second_ref)
    new = [ref[...] - fast_step * value for ref, value in zip(old, last)]
    for ref, value in zip((new_first_ref, new_third_ref, new_second_ref), new):
        ref[...] = value
    narrow = [weight.astype(BF) for weight in new]
    normed_ref[...] = applied(qkv_ref[1, :, :512], *narrow, gain_ref[...])


ROWS = 128


def scores(place, queries_ref, own, swap_one, one, swap_two, two, out_ref, sum_ref, held):
    z, index, core = place[0], place[1], place[2]
    for tile in range(SUPER // ROWS):
        queries = queries_ref[tile * ROWS : (tile + 1) * ROWS]
        query_at = (
            ((tile // 2) ^ z) * HALF
            + (tile % 2) * ROWS
            + lax.broadcasted_iota(jnp.int32, (ROWS, SUPER), 0)
        )
        column = lax.broadcasted_iota(jnp.int32, (ROWS, SUPER), 1)
        highest = jnp.full((ROWS, 1), MASKED, F32)
        order = ((own, 0), (one, 2), (two, REACH), (swap_one, 1 + 2 * core), (swap_two, 3 - 2 * core))
        for slot, (piece, distance) in enumerate(order):
            source = z * 16 + index - distance
            part = nt(queries, piece[...]) * (512 ** (-0.5))
            if slot == 0:
                shift = z * HALF
                key_at = jnp.where(column < HALF, column + shift, column - shift)
                part = jnp.where(key_at <= query_at, part, MASKED)
            elif slot == 2:
                shift = jnp.where(source >= 16, HALF, 0)
                key_at = jnp.where(column < HALF, column + shift, column - shift)
                part = jnp.where((key_at > query_at) & (source >= 0), part, MASKED)
            else:
                part = jnp.where(source >= 0, part, MASKED)
            held[slot] = part
            highest = jnp.maximum(highest, jnp.max(part, axis=1, keepdims=True))
        total = jnp.zeros((ROWS, 1), F32)
        rows = slice(tile * ROWS, (tile + 1) * ROWS)
        for slot in range(5):
            weights = jnp.exp(held[slot] - highest)
            total = total + jnp.sum(weights, axis=1, keepdims=True)
            out_ref[slot, rows] = weights.astype(BF)
        sum_ref[rows] = jnp.broadcast_to(1.0 / total, (ROWS, 128))


def gathered(weights_ref, sum_ref, own, swap_one, one, swap_two, two, same_ref, other_ref):
    for half, out_ref in enumerate((same_ref, other_ref)):
        rows = slice(half * HALF, (half + 1) * HALF)
        result = jnp.zeros((HALF, 512), F32)
        for slot, piece in enumerate((own, one, two, swap_one, swap_two)):
            result = result + nn(weights_ref[slot, rows], piece[...])
        out_ref[...] = (result * sum_ref[rows, 0:1]).astype(BF)


def mix(place, near_ref, far_ref, normed_ref, w_ref, keep_ref, send_ref, *, block_num):
    z, core, pair = place[0], place[2], place[3]
    attended = jnp.where(z == block_num, near_ref[...], far_ref[...])
    combined = (attended.astype(F32) + normed_ref[...]).astype(BF)
    for step in range(2):
        for out_ref, whose in ((keep_ref, core), (send_ref, 1 - core)):
            column = pl.multiple_of(((pair ^ step) * 2 + whose) * 512, 512)
            out_ref[step] = nn(combined, w_ref[:, pl.ds(column, 512)]).astype(BF)


def mix_zero(*refs):
    mix(*refs, block_num=0)


def mix_one(*refs):
    mix(*refs, block_num=1)


def mixed_by(kernel, place, near, far, normed, w_out):
    return call(kernel, [smem()] + [vmem()] * 4, [((2, HALF, 512), BF)] * 2)(
        place, near, far, normed, w_out
    )


def ordered(values, *before):
    kept = lax.optimization_barrier((tuple(values), before))
    return list(kept[0])


def exchanged(pieces, axis):
    received = [pieces[0]]
    for step in range(1, len(pieces)):
        dx, dy, dz = (step if axis == name else 0 for name in "xyz")

        def route(x, y, z, zh, core):
            return (x ^ dx, y ^ dy, z ^ dz, zh, core)

        received.append(moved(pieces[step], route))
    return received


def shards(tokens, w_qkv, w_rate, w_out, fw_gain, fast_first, fast_third, fast_second):
    width = tokens.shape[2]
    ctx, head = lax.axis_index("ctx"), lax.axis_index("head")
    x, y, z = ctx // 8, (ctx // 2) % 4, ctx % 2
    zh, core = head // 2, head % 2
    index = 4 * x + (y & 2) + core
    place = jnp.stack([z, index, core, zh, x, y]).astype(jnp.int32)
    first, third, second = fast_first[0], fast_third[0], fast_second[0]

    natural, same, other = run_project(
        place, tokens, w_qkv.reshape(width, 1536)
    )
    same = moved(same, to_role_same)
    other = moved(other, to_role_other)
    grads = call(
        fast_grads,
        [smem()] + [vmem()] * 6,
        [((384, 512), BF)] * 4,
        scratch=(pltpu.VMEM((1536, 512), BF),),
        limit=24,
    )(place, tokens, w_rate.reshape(1, width), natural, first, third, second)
    same, other = ordered([same, other], *grads)
    grads = exchanged(grads, "x")
    queries, own_keys, own_values = (
        jnp.concatenate([half[at * HALF : (at + 1) * HALF] for half in (same, other)], axis=0)
        for at in range(3)
    )
    grads = call(
        reduce_x,
        [smem()] + [vmem()] * 4,
        [((96, 512), BF)] * 4,
        scratch=(pltpu.VMEM((384, 512), BF),),
    )(place, *grads)
    (own_keys,) = ordered([own_keys], grads[0])
    two_keys = moved(own_keys, quads_on(2))
    grads = exchanged(grads, "y")
    (piece,) = call(reduce_y, [vmem()] * 4, [((96, 512), BF)])(*grads)
    (own_values,) = ordered([own_values], piece)
    two_values = moved(own_values, quads_on(2))
    (piece,) = call(reduce_z, [vmem()] * 2, [((96, 512), BF)])(*exchanged([piece] * 2, "z"))

    def onward(own, two):
        return jnp.where(y >= 2, two, own), jnp.where(core == 0, own, two)

    (two_keys,) = ordered([two_keys], piece)
    one_keys, swap_two_keys = onward(own_keys, two_keys)
    piece = exchanged([piece] * 4, "y")
    piece = jnp.concatenate(ordered(piece, one_keys), axis=0)
    one_keys = moved(one_keys, across)
    swap_two_keys = moved(swap_two_keys, other_core)
    lines = [[8 * at_x + at for at_x in range(CTX_X)] for at in range(8)]
    sent = jnp.broadcast_to(piece[None], (CTX_X, 384, 512))
    parts = [lax.all_to_all(sent, "ctx", 0, 0, axis_index_groups=lines, tiled=True)]
    (two_values,) = ordered([two_values], sent)
    one_values, swap_two_values = onward(own_values, two_values)
    (queries,) = ordered([queries], piece)
    one_values = moved(one_values, across)
    swap_two_values = moved(swap_two_values, other_core)

    swap_one_keys = moved(one_keys, other_core)
    weights, sums = call(
        scores,
        [smem()] + [vmem()] * 6,
        [((5, SUPER, SUPER), BF), ((SUPER, 128), F32)],
        scratch=(pltpu.VMEM((5, ROWS, SUPER), F32),),
    )(place, queries, own_keys, swap_one_keys, one_keys, swap_two_keys, two_keys)
    (one_values,) = ordered([one_values], weights)
    swap_one_values = moved(one_values, other_core)
    near, far = call(gathered, [vmem()] * 7, [((HALF, 512), BF)] * 2)(
        weights, sums, own_values, swap_one_values, one_values, swap_two_values, two_values
    )
    parts = ordered(parts, near, far)
    near = moved(near, to_role_same)
    far = moved(far, to_role_other)

    (normed_zero,) = call(
        fast_apply, [vmem()] * 5, [((HALF, 512), F32)]
    )(natural, first, third, second, fw_gain)
    normed_zero, near, far = ordered([normed_zero, near, far], *parts)
    (held,) = call(
        update_start,
        [smem(), vmem()],
        [((3, 512, 512), BF)],
        scratch=(pltpu.VMEM((1536, 512), BF),),
        limit=24,
    )(place, *parts)
    (normed_zero,) = ordered([normed_zero], held)
    keep, send = mixed_by(mix_zero, place, near, far, normed_zero, w_out[0])
    (held,) = ordered([held], send)
    taken = moved(send, other_core)
    (held,) = call(update_middle, [vmem()], [((3, 512, 512), BF)], limit=24)(held)
    (taken,) = ordered([taken], held)
    half_zero = keep.astype(F32) + taken.astype(F32)
    crossing = half_zero[1].astype(BF)
    (held,) = ordered([held], crossing)
    crossing = moved(crossing, other_pair)
    new_first, new_third, new_second, normed_one = call(
        update_end,
        [vmem()] * 6,
        [((512, 512), F32)] * 3 + [((HALF, 512), F32)],
        scratch=(pltpu.VMEM((3, 512, 512), BF),),
        limit=24,
    )(held, first, third, second, natural, fw_gain)
    (normed_one,) = ordered([normed_one], crossing)
    keep, send = mixed_by(mix_one, place, near, far, normed_one, w_out[0])
    half_one = keep.astype(F32) + moved(send, other_core).astype(F32)
    done_zero = half_zero[0] + crossing.astype(F32)
    done_one = half_one[0] + moved(half_one[1].astype(BF), other_pair).astype(F32)
    mixed = jnp.stack([done_zero, done_one]).astype(BF)
    return (mixed, new_first[None], new_third[None], new_second[None])


def solution(mesh):
    placed = (
        P(None, "ctx", None),
        P(None, "head", None),
        P(None, "head"),
        P("head", None, None),
        P("head", None),
        P("head", None, None),
        P("head", None, None),
        P("head", None, None),
    )
    return jax.shard_map(
        shards,
        mesh=mesh,
        in_specs=placed,
        out_specs=(
            P(None, "ctx", "head"),
            P("head", None, None),
            P("head", None, None),
            P("head", None, None),
        ),
        check_vma=False,
    )
```

```python
import jax
import jax.numpy as jnp
from jax import lax
from jax.experimental import pallas as pl
from jax.experimental.pallas import tpu as pltpu
from jax.sharding import PartitionSpec as P

NS_STEPS = 5
FIRST_STEPS = 1
MIDDLE_STEPS = 2
HALF = 256
SUPER = 512
REACH = 4
BF = jnp.bfloat16
F32 = jnp.float32

coeff_a = 3.4445
coeff_b = -4.775
coeff_c = 2.0315
fast_step = 0.5
norm_eps = 1e-06
MASKED = -1e30

CTX_X, CTX_Y, CTX_Z = 4, 4, 2


def nn(left, right):
    return lax.dot_general(left, right, (((1,), (0,)), ((), ())), preferred_element_type=F32)


def nt(left, right):
    return lax.dot_general(left, right, (((1,), (1,)), ((), ())), preferred_element_type=F32)


def tn(left, right):
    return lax.dot_general(left, right, (((0,), (0,)), ((), ())), preferred_element_type=F32)


def moved(value, route):
    pairs = []
    for ctx in range(CTX_X * CTX_Y * CTX_Z):
        x, y, z = ctx // 8, (ctx // 2) % 4, ctx % 2
        for head in range(4):
            target = route(x, y, z, head // 2, head % 2)
            if target is not None:
                tx, ty, tz, th, tc = target
                pairs.append((ctx * 4 + head, (tx * 8 + ty * 2 + tz) * 4 + th * 2 + tc))
    return lax.ppermute(value, ("ctx", "head"), pairs)


def to_role_same(x, y, z, zh, core):
    return (x, (y & 2) + core, z, zh, y & 1)


def to_role_other(x, y, z, zh, core):
    return (x, (y & 2) + core, 1 - z, zh, y & 1)


def quads_on(steps):
    def route(x, y, z, zh, core):
        place = z * 8 + 2 * x + (y >> 1) + steps
        if place >= 16:
            return None
        quad = place % 8
        return (quad // 2, (quad % 2) * 2 + (y & 1), place // 8, zh, core)

    return route


def across(x, y, z, zh, core):
    return (x, y ^ 2, z, zh, core)


def other_core(x, y, z, zh, core):
    return (x, y, z, zh, 1 - core)


def other_pair(x, y, z, zh, core):
    return (x, y, z, 1 - zh, core)


def vmem():
    return pl.BlockSpec(memory_space=pltpu.VMEM)


def smem():
    return pl.BlockSpec(memory_space=pltpu.SMEM)


def call(kernel, specs, outs, flops=1 << 20, scratch=(), limit=16):
    return pl.pallas_call(
        kernel,
        in_specs=specs,
        out_specs=[vmem()] * len(outs),
        out_shape=[jax.ShapeDtypeStruct(shape, dtype) for shape, dtype in outs],
        scratch_shapes=list(scratch),
        compiler_params=pltpu.CompilerParams(vmem_limit_bytes=limit << 20),
        cost_estimate=pl.CostEstimate(flops=flops, bytes_accessed=1 << 10, transcendentals=0),
        name=kernel.__name__,
    )


CHUNKS = 4
DEPTH = 512


def project(place, tokens_ref, w_ref, natural_ref, same, other, tokens_held, held, total, sems):
    copies = []
    for j in range(CHUNKS):
        rows = pl.ds(j * DEPTH, DEPTH)
        copies.append(
            (
                pltpu.make_async_copy(
                    tokens_ref.at[:, :, rows], tokens_held.at[:, :, rows], sems.at[CHUNKS + j]
                ),
                pltpu.make_async_copy(w_ref.at[rows], held.at[rows], sems.at[j]),
            )
        )
    for pair in copies:
        for copy in pair:
            copy.start()
    z = place[0]
    for j, pair in enumerate(copies):
        for copy in pair:
            copy.wait()
        depth = slice(j * DEPTH, (j + 1) * DEPTH)
        tokens = tokens_held[:, :, depth].reshape(2 * HALF, DEPTH)
        for at in range(3):
            columns = slice(at * 512, (at + 1) * 512)
            part = nn(tokens, held[depth, columns])
            if j == 0:
                total[:, columns] = part
            elif j < CHUNKS - 1:
                total[:, columns] += part
            else:
                result = (total[:, columns] + part).astype(BF)
                low, high = result[:HALF], result[HALF:]
                natural_ref[0, :, columns] = low
                natural_ref[1, :, columns] = high
                rows = slice(at * HALF, (at + 1) * HALF)
                same[rows] = jnp.where(z == 0, low, high)
                other[rows] = jnp.where(z == 0, high, low)


def run_project(place, tokens, weights):
    return call(
        project,
        [smem()] + [pl.BlockSpec(memory_space=pltpu.HBM)] * 2,
        [((2, HALF, 1536), BF)] + [((3 * HALF, 512), BF)] * 2,
        scratch=(
            pltpu.VMEM((2, HALF, 2048), BF),
            pltpu.VMEM((2048, 1536), BF),
            pltpu.VMEM((SUPER, 1536), F32),
            pltpu.SemaphoreType.DMA((2 * CHUNKS,)),
        ),
        limit=50,
    )(place, tokens, weights)


def spread(whole, outs, at):
    rows = outs[0].shape[0]
    for step, ref in enumerate(outs):
        start = pl.multiple_of((at ^ step) * rows, rows)
        ref[...] = whole[pl.ds(start, rows)]


def fast_grads(place, tokens_ref, rate_ref, qkv_ref, first_ref, third_ref, second_ref, *rest):
    out_ref = rest[4]
    drive = jnp.sum(
        tokens_ref[0].astype(F32) * rate_ref[...].astype(F32), axis=1, keepdims=True
    )
    rates = jnp.maximum(drive, 0.0) + jnp.log1p(jnp.exp(-jnp.abs(drive)))
    keys = qkv_ref[0, :, 512:1024]
    values = qkv_ref[0, :, 1024:]
    hidden_one = nn(keys, first_ref[...].astype(BF))
    hidden_three = nn(keys, third_ref[...].astype(BF))
    target = (-rates * values.astype(F32)).astype(BF)
    dactiv = nt(target, second_ref[...].astype(BF))
    sigma = jax.nn.sigmoid(hidden_one)
    silu = hidden_one * sigma
    activ = (silu * hidden_three).astype(BF)
    d_first = (dactiv * hidden_three * (sigma * (1.0 + hidden_one * (1.0 - sigma)))).astype(BF)
    d_third = (dactiv * silu).astype(BF)
    out_ref[0:512] = tn(keys, d_first).astype(BF)
    out_ref[512:1024] = tn(keys, d_third).astype(BF)
    out_ref[1024:1536] = tn(activ, target).astype(BF)
    spread(out_ref, rest[:4], place[4])


def summed(refs):
    total = refs[0][...].astype(F32)
    for ref in refs[1:]:
        total = total + ref[...].astype(F32)
    return total.astype(BF)


def reduce_x(place, *refs):
    refs[8][...] = summed(refs[:4])
    spread(refs[8], refs[4:8], place[5])


def reduce_y(*refs):
    refs[4][...] = summed(refs[:4])


def reduce_z(*refs):
    refs[2][...] = summed(refs[:2])


def applied(queries, first, third, second, gain):
    hidden_one = nn(queries, first)
    hidden_three = nn(queries, third)
    activ = (jax.nn.silu(hidden_one) * hidden_three).astype(BF)
    fast_out = nn(activ, second)
    mean = jnp.mean(fast_out * fast_out, axis=1, keepdims=True)
    return fast_out * lax.rsqrt(mean + norm_eps) * gain


def fast_apply(qkv_ref, first_ref, third_ref, second_ref, gain_ref, out_ref):
    out_ref[...] = applied(
        qkv_ref[0, :, :512],
        first_ref[...].astype(BF),
        third_ref[...].astype(BF),
        second_ref[...].astype(BF),
        gain_ref[...],
    )


def advanced(now):
    grams = [nt(x, x) for x in now]
    narrow = [gram.astype(BF) for gram in grams]
    polys = [
        (coeff_b * gram + coeff_c * nn(low, low)).astype(BF)
        for gram, low in zip(grams, narrow)
    ]
    return [coeff_a * x.astype(F32) + nn(poly, x) for x, poly in zip(now, polys)]


def repeated(ref, steps):
    @pl.loop(0, steps)
    def _(step):
        for which, value in enumerate(advanced([ref[which] for which in range(3)])):
            ref[which] = value.astype(BF)


def update_start(place, parts_ref, out_ref, grad_ref):
    y = place[5]
    for at_x in range(4):
        for across_y in range(4):
            start = at_x * 384 + (y ^ across_y) * 96
            at = across_y * 96
            grad_ref[pl.ds(pl.multiple_of(start, 96), 96)] = parts_ref[
                at_x, at : at + 96
            ]
    for which in range(3):
        grad = grad_ref[which * 512 : (which + 1) * 512].astype(F32)
        scale = lax.rsqrt(jnp.sum(grad * grad, keepdims=True) + norm_eps)
        out_ref[which] = (grad * scale).astype(BF)
    repeated(out_ref, FIRST_STEPS)


def update_middle(in_ref, out_ref):
    out_ref[...] = in_ref[...]
    repeated(out_ref, MIDDLE_STEPS)


def update_end(
    in_ref,
    first_ref,
    third_ref,
    second_ref,
    qkv_ref,
    gain_ref,
    new_first_ref,
    new_third_ref,
    new_second_ref,
    normed_ref,
    held,
):
    held[...] = in_ref[...]
    repeated(held, NS_STEPS - 1 - FIRST_STEPS - MIDDLE_STEPS)
    last = advanced([held[which] for which in range(3)])
    old = (first_ref, third_ref, second_ref)
    new = [ref[...] - fast_step * value for ref, value in zip(old, last)]
    for ref, value in zip((new_first_ref, new_third_ref, new_second_ref), new):
        ref[...] = value
    narrow = [weight.astype(BF) for weight in new]
    normed_ref[...] = applied(qkv_ref[1, :, :512], *narrow, gain_ref[...])


ROWS = 128


def scores(place, queries_ref, own, swap_one, one, swap_two, two, out_ref, sum_ref, held):
    z, index, core = place[0], place[1], place[2]
    for tile in range(SUPER // ROWS):
        queries = queries_ref[tile * ROWS : (tile + 1) * ROWS]
        query_at = (
            ((tile // 2) ^ z) * HALF
            + (tile % 2) * ROWS
            + lax.broadcasted_iota(jnp.int32, (ROWS, SUPER), 0)
        )
        column = lax.broadcasted_iota(jnp.int32, (ROWS, SUPER), 1)
        highest = jnp.full((ROWS, 1), MASKED, F32)
        order = ((own, 0), (one, 2), (two, REACH), (swap_one, 1 + 2 * core), (swap_two, 3 - 2 * core))
        for slot, (piece, distance) in enumerate(order):
            source = z * 16 + index - distance
            part = nt(queries, piece[...]) * (512 ** (-0.5))
            if slot == 0:
                shift = z * HALF
                key_at = jnp.where(column < HALF, column + shift, column - shift)
                part = jnp.where(key_at <= query_at, part, MASKED)
            elif slot == 2:
                shift = jnp.where(source >= 16, HALF, 0)
                key_at = jnp.where(column < HALF, column + shift, column - shift)
                part = jnp.where((key_at > query_at) & (source >= 0), part, MASKED)
            else:
                part = jnp.where(source >= 0, part, MASKED)
            held[slot] = part
            highest = jnp.maximum(highest, jnp.max(part, axis=1, keepdims=True))
        total = jnp.zeros((ROWS, 1), F32)
        rows = slice(tile * ROWS, (tile + 1) * ROWS)
        for slot in range(5):
            weights = jnp.exp(held[slot] - highest)
            total = total + jnp.sum(weights, axis=1, keepdims=True)
            out_ref[slot, rows] = weights.astype(BF)
        sum_ref[rows] = jnp.broadcast_to(1.0 / total, (ROWS, 128))


def gathered(weights_ref, sum_ref, own, swap_one, one, swap_two, two, same_ref, other_ref):
    for half, out_ref in enumerate((same_ref, other_ref)):
        rows = slice(half * HALF, (half + 1) * HALF)
        result = jnp.zeros((HALF, 512), F32)
        for slot, piece in enumerate((own, one, two, swap_one, swap_two)):
            result = result + nn(weights_ref[slot, rows], piece[...])
        out_ref[...] = (result * sum_ref[rows, 0:1]).astype(BF)


def mix(place, near_ref, far_ref, normed_ref, w_ref, keep_ref, send_ref, *, block_num):
    z, core, pair = place[0], place[2], place[3]
    attended = jnp.where(z == block_num, near_ref[...], far_ref[...])
    combined = (attended.astype(F32) + normed_ref[...]).astype(BF)
    for step in range(2):
        for out_ref, whose in ((keep_ref, core), (send_ref, 1 - core)):
            column = pl.multiple_of(((pair ^ step) * 2 + whose) * 512, 512)
            out_ref[step] = nn(combined, w_ref[:, pl.ds(column, 512)]).astype(BF)


def mix_zero(*refs):
    mix(*refs, block_num=0)


def mix_one(*refs):
    mix(*refs, block_num=1)


def mixed_by(kernel, place, near, far, normed, w_out):
    return call(kernel, [smem()] + [vmem()] * 4, [((2, HALF, 512), BF)] * 2)(
        place, near, far, normed, w_out
    )


def ordered(values, *before):
    kept = lax.optimization_barrier((tuple(values), before))
    return list(kept[0])


def exchanged(pieces, axis):
    received = [pieces[0]]
    for step in range(1, len(pieces)):
        dx, dy, dz = (step if axis == name else 0 for name in "xyz")

        def route(x, y, z, zh, core):
            return (x ^ dx, y ^ dy, z ^ dz, zh, core)

        received.append(moved(pieces[step], route))
    return received


def shards(tokens, w_qkv, w_rate, w_out, fw_gain, fast_first, fast_third, fast_second):
    width = tokens.shape[2]
    ctx, head = lax.axis_index("ctx"), lax.axis_index("head")
    x, y, z = ctx // 8, (ctx // 2) % 4, ctx % 2
    zh, core = head // 2, head % 2
    index = 4 * x + (y & 2) + core
    place = jnp.stack([z, index, core, zh, x, y]).astype(jnp.int32)
    first, third, second = fast_first[0], fast_third[0], fast_second[0]

    natural, same, other = run_project(
        place, tokens, w_qkv.reshape(width, 1536)
    )
    same = moved(same, to_role_same)
    other = moved(other, to_role_other)
    grads = call(
        fast_grads,
        [smem()] + [vmem()] * 6,
        [((384, 512), BF)] * 4,
        scratch=(pltpu.VMEM((1536, 512), BF),),
        limit=24,
    )(place, tokens, w_rate.reshape(1, width), natural, first, third, second)
    same, other = ordered([same, other], *grads)
    grads = exchanged(grads, "x")
    queries, own_keys, own_values = (
        jnp.concatenate([half[at * HALF : (at + 1) * HALF] for half in (same, other)], axis=0)
        for at in range(3)
    )
    grads = call(
        reduce_x,
        [smem()] + [vmem()] * 4,
        [((96, 512), BF)] * 4,
        scratch=(pltpu.VMEM((384, 512), BF),),
    )(place, *grads)
    (own_keys,) = ordered([own_keys], grads[0])
    two_keys = moved(own_keys, quads_on(2))
    grads = exchanged(grads, "y")
    (piece,) = call(reduce_y, [vmem()] * 4, [((96, 512), BF)])(*grads)
    (own_values,) = ordered([own_values], piece)
    two_values = moved(own_values, quads_on(2))
    (piece,) = call(reduce_z, [vmem()] * 2, [((96, 512), BF)])(*exchanged([piece] * 2, "z"))

    def onward(own, two):
        return jnp.where(y >= 2, two, own), jnp.where(core == 0, own, two)

    (two_keys,) = ordered([two_keys], piece)
    one_keys, swap_two_keys = onward(own_keys, two_keys)
    piece = exchanged([piece] * 4, "y")
    piece = jnp.concatenate(ordered(piece, one_keys), axis=0)
    one_keys = moved(one_keys, across)
    swap_two_keys = moved(swap_two_keys, other_core)
    lines = [[8 * at_x + at for at_x in range(CTX_X)] for at in range(8)]
    sent = jnp.broadcast_to(piece[None], (CTX_X, 384, 512))
    parts = [lax.all_to_all(sent, "ctx", 0, 0, axis_index_groups=lines, tiled=True)]
    (two_values,) = ordered([two_values], sent)
    one_values, swap_two_values = onward(own_values, two_values)
    (queries,) = ordered([queries], piece)
    one_values = moved(one_values, across)
    swap_two_values = moved(swap_two_values, other_core)

    swap_one_keys = moved(one_keys, other_core)
    weights, sums = call(
        scores,
        [smem()] + [vmem()] * 6,
        [((5, SUPER, SUPER), BF), ((SUPER, 128), F32)],
        scratch=(pltpu.VMEM((5, ROWS, SUPER), F32),),
    )(place, queries, own_keys, swap_one_keys, one_keys, swap_two_keys, two_keys)
    parts = ordered(parts, weights)
    (held,) = call(
        update_start,
        [smem(), vmem()],
        [((3, 512, 512), BF)],
        scratch=(pltpu.VMEM((1536, 512), BF),),
        limit=24,
    )(place, *parts)
    (one_values,) = ordered([one_values], weights, held)
    swap_one_values = moved(one_values, other_core)
    near, far = call(gathered, [vmem()] * 7, [((HALF, 512), BF)] * 2)(
        weights, sums, own_values, swap_one_values, one_values, swap_two_values, two_values
    )
    (held,) = ordered([held], near, far)
    near = moved(near, to_role_same)
    far = moved(far, to_role_other)

    (normed_zero,) = call(
        fast_apply, [vmem()] * 5, [((HALF, 512), F32)]
    )(natural, first, third, second, fw_gain)
    (held,) = call(update_middle, [vmem()], [((3, 512, 512), BF)], limit=24)(held)
    normed_zero, near, far = ordered([normed_zero, near, far], held)
    keep, send = mixed_by(mix_zero, place, near, far, normed_zero, w_out[0])
    (held,) = ordered([held], send)
    taken = moved(send, other_core)
    new_first, new_third, new_second, normed_one = call(
        update_end,
        [vmem()] * 6,
        [((512, 512), F32)] * 3 + [((HALF, 512), F32)],
        scratch=(pltpu.VMEM((3, 512, 512), BF),),
        limit=24,
    )(held, first, third, second, natural, fw_gain)
    (taken,) = ordered([taken], normed_one)
    half_zero = keep.astype(F32) + taken.astype(F32)
    crossing = half_zero[1].astype(BF)
    (normed_one,) = ordered([normed_one], crossing)
    crossing = moved(crossing, other_pair)
    keep, send = mixed_by(mix_one, place, near, far, normed_one, w_out[0])
    half_one = keep.astype(F32) + moved(send, other_core).astype(F32)
    done_zero = half_zero[0] + crossing.astype(F32)
    done_one = half_one[0] + moved(half_one[1].astype(BF), other_pair).astype(F32)
    mixed = jnp.stack([done_zero, done_one]).astype(BF)
    return (mixed, new_first[None], new_third[None], new_second[None])


def solution(mesh):
    placed = (
        P(None, "ctx", None),
        P(None, "head", None),
        P(None, "head"),
        P("head", None, None),
        P("head", None),
        P("head", None, None),
        P("head", None, None),
        P("head", None, None),
    )
    return jax.shard_map(
        shards,
        mesh=mesh,
        in_specs=placed,
        out_specs=(
            P(None, "ctx", "head"),
            P("head", None, None),
            P("head", None, None),
            P("head", None, None),
        ),
        check_vma=False,
    )
```

```python
import jax
import jax.numpy as jnp
from jax import lax
from jax.experimental import pallas as pl
from jax.experimental.pallas import tpu as pltpu
from jax.sharding import PartitionSpec as P

NS_STEPS = 5
FIRST_STEPS = 1
MIDDLE_STEPS = 2
HALF = 256
SUPER = 512
REACH = 4
BF = jnp.bfloat16
F32 = jnp.float32

coeff_a = 3.4445
coeff_b = -4.775
coeff_c = 2.0315
fast_step = 0.5
norm_eps = 1e-06
MASKED = -1e30

CTX_X, CTX_Y, CTX_Z = 4, 4, 2


def nn(left, right):
    return lax.dot_general(left, right, (((1,), (0,)), ((), ())), preferred_element_type=F32)


def nt(left, right):
    return lax.dot_general(left, right, (((1,), (1,)), ((), ())), preferred_element_type=F32)


def tn(left, right):
    return lax.dot_general(left, right, (((0,), (0,)), ((), ())), preferred_element_type=F32)


def moved(value, route):
    pairs = []
    for ctx in range(CTX_X * CTX_Y * CTX_Z):
        x, y, z = ctx // 8, (ctx // 2) % 4, ctx % 2
        for head in range(4):
            target = route(x, y, z, head // 2, head % 2)
            if target is not None:
                tx, ty, tz, th, tc = target
                pairs.append((ctx * 4 + head, (tx * 8 + ty * 2 + tz) * 4 + th * 2 + tc))
    return lax.ppermute(value, ("ctx", "head"), pairs)


def to_role_same(x, y, z, zh, core):
    return (x, (y & 2) + core, z, zh, y & 1)


def to_role_other(x, y, z, zh, core):
    return (x, (y & 2) + core, 1 - z, zh, y & 1)


def quads_on(steps):
    def route(x, y, z, zh, core):
        place = z * 8 + 2 * x + (y >> 1) + steps
        if place >= 16:
            return None
        quad = place % 8
        return (quad // 2, (quad % 2) * 2 + (y & 1), place // 8, zh, core)

    return route


def across(x, y, z, zh, core):
    return (x, y ^ 2, z, zh, core)


def other_core(x, y, z, zh, core):
    return (x, y, z, zh, 1 - core)


def other_pair(x, y, z, zh, core):
    return (x, y, z, 1 - zh, core)


def vmem():
    return pl.BlockSpec(memory_space=pltpu.VMEM)


def smem():
    return pl.BlockSpec(memory_space=pltpu.SMEM)


def call(kernel, specs, outs, flops=1 << 20, scratch=(), limit=16):
    return pl.pallas_call(
        kernel,
        in_specs=specs,
        out_specs=[vmem()] * len(outs),
        out_shape=[jax.ShapeDtypeStruct(shape, dtype) for shape, dtype in outs],
        scratch_shapes=list(scratch),
        compiler_params=pltpu.CompilerParams(vmem_limit_bytes=limit << 20),
        cost_estimate=pl.CostEstimate(flops=flops, bytes_accessed=1 << 10, transcendentals=0),
        name=kernel.__name__,
    )


CHUNKS = 4
DEPTH = 512


def project(place, tokens_ref, w_ref, natural_ref, same, other, tokens_held, held, total, sems):
    copies = []
    for j in range(CHUNKS):
        rows = pl.ds(j * DEPTH, DEPTH)
        copies.append(
            (
                pltpu.make_async_copy(
                    tokens_ref.at[:, :, rows], tokens_held.at[:, :, rows], sems.at[CHUNKS + j]
                ),
                pltpu.make_async_copy(w_ref.at[rows], held.at[rows], sems.at[j]),
            )
        )
    for pair in copies:
        for copy in pair:
            copy.start()
    z = place[0]
    for j, pair in enumerate(copies):
        for copy in pair:
            copy.wait()
        depth = slice(j * DEPTH, (j + 1) * DEPTH)
        tokens = tokens_held[:, :, depth].reshape(2 * HALF, DEPTH)
        for at in range(3):
            columns = slice(at * 512, (at + 1) * 512)
            part = nn(tokens, held[depth, columns])
            if j == 0:
                total[:, columns] = part
            elif j < CHUNKS - 1:
                total[:, columns] += part
            else:
                result = (total[:, columns] + part).astype(BF)
                low, high = result[:HALF], result[HALF:]
                natural_ref[0, :, columns] = low
                natural_ref[1, :, columns] = high
                rows = slice(at * HALF, (at + 1) * HALF)
                same[rows] = jnp.where(z == 0, low, high)
                other[rows] = jnp.where(z == 0, high, low)


def run_project(place, tokens, weights):
    return call(
        project,
        [smem()] + [pl.BlockSpec(memory_space=pltpu.HBM)] * 2,
        [((2, HALF, 1536), BF)] + [((3 * HALF, 512), BF)] * 2,
        scratch=(
            pltpu.VMEM((2, HALF, 2048), BF),
            pltpu.VMEM((2048, 1536), BF),
            pltpu.VMEM((SUPER, 1536), F32),
            pltpu.SemaphoreType.DMA((2 * CHUNKS,)),
        ),
        limit=50,
    )(place, tokens, weights)


def spread(whole, outs, at):
    rows = outs[0].shape[0]
    for step, ref in enumerate(outs):
        start = pl.multiple_of((at ^ step) * rows, rows)
        ref[...] = whole[pl.ds(start, rows)]


def fast_grads(place, tokens_ref, rate_ref, qkv_ref, first_ref, third_ref, second_ref, *rest):
    out_ref = rest[4]
    drive = jnp.sum(
        tokens_ref[0].astype(F32) * rate_ref[...].astype(F32), axis=1, keepdims=True
    )
    rates = jnp.maximum(drive, 0.0) + jnp.log1p(jnp.exp(-jnp.abs(drive)))
    keys = qkv_ref[0, :, 512:1024]
    values = qkv_ref[0, :, 1024:]
    hidden_one = nn(keys, first_ref[...].astype(BF))
    hidden_three = nn(keys, third_ref[...].astype(BF))
    target = (-rates * values.astype(F32)).astype(BF)
    dactiv = nt(target, second_ref[...].astype(BF))
    sigma = jax.nn.sigmoid(hidden_one)
    silu = hidden_one * sigma
    activ = (silu * hidden_three).astype(BF)
    d_first = (dactiv * hidden_three * (sigma * (1.0 + hidden_one * (1.0 - sigma)))).astype(BF)
    d_third = (dactiv * silu).astype(BF)
    out_ref[0:512] = tn(keys, d_first).astype(BF)
    out_ref[512:1024] = tn(keys, d_third).astype(BF)
    out_ref[1024:1536] = tn(activ, target).astype(BF)
    spread(out_ref, rest[:4], place[4])


def summed(refs):
    total = refs[0][...].astype(F32)
    for ref in refs[1:]:
        total = total + ref[...].astype(F32)
    return total.astype(BF)


def reduce_x(place, *refs):
    refs[8][...] = summed(refs[:4])
    spread(refs[8], refs[4:8], place[5])


def reduce_y(*refs):
    refs[4][...] = summed(refs[:4])


def reduce_z(*refs):
    refs[2][...] = summed(refs[:2])


def applied(queries, first, third, second, gain):
    hidden_one = nn(queries, first)
    hidden_three = nn(queries, third)
    activ = (jax.nn.silu(hidden_one) * hidden_three).astype(BF)
    fast_out = nn(activ, second)
    mean = jnp.mean(fast_out * fast_out, axis=1, keepdims=True)
    return fast_out * lax.rsqrt(mean + norm_eps) * gain


def fast_apply(qkv_ref, first_ref, third_ref, second_ref, gain_ref, out_ref):
    out_ref[...] = applied(
        qkv_ref[0, :, :512],
        first_ref[...].astype(BF),
        third_ref[...].astype(BF),
        second_ref[...].astype(BF),
        gain_ref[...],
    )


def advanced(now):
    grams = [nt(x, x) for x in now]
    narrow = [gram.astype(BF) for gram in grams]
    polys = [
        (coeff_b * gram + coeff_c * nn(low, low)).astype(BF)
        for gram, low in zip(grams, narrow)
    ]
    return [coeff_a * x.astype(F32) + nn(poly, x) for x, poly in zip(now, polys)]


def repeated(ref, steps):
    @pl.loop(0, steps)
    def _(step):
        for which, value in enumerate(advanced([ref[which] for which in range(3)])):
            ref[which] = value.astype(BF)


def update_start(place, parts_ref, out_ref, grad_ref):
    y = place[5]
    for at_x in range(4):
        for across_y in range(4):
            start = at_x * 384 + (y ^ across_y) * 96
            at = across_y * 96
            grad_ref[pl.ds(pl.multiple_of(start, 96), 96)] = parts_ref[
                at_x, at : at + 96
            ]
    for which in range(3):
        grad = grad_ref[which * 512 : (which + 1) * 512].astype(F32)
        scale = lax.rsqrt(jnp.sum(grad * grad, keepdims=True) + norm_eps)
        out_ref[which] = (grad * scale).astype(BF)
    repeated(out_ref, FIRST_STEPS)


def update_middle(in_ref, out_ref):
    out_ref[...] = in_ref[...]
    repeated(out_ref, MIDDLE_STEPS)


def update_end(
    in_ref,
    first_ref,
    third_ref,
    second_ref,
    qkv_ref,
    gain_ref,
    new_first_ref,
    new_third_ref,
    new_second_ref,
    normed_ref,
    held,
):
    held[...] = in_ref[...]
    repeated(held, NS_STEPS - 1 - FIRST_STEPS - MIDDLE_STEPS)
    last = advanced([held[which] for which in range(3)])
    old = (first_ref, third_ref, second_ref)
    new = [ref[...] - fast_step * value for ref, value in zip(old, last)]
    for ref, value in zip((new_first_ref, new_third_ref, new_second_ref), new):
        ref[...] = value
    narrow = [weight.astype(BF) for weight in new]
    normed_ref[...] = applied(qkv_ref[1, :, :512], *narrow, gain_ref[...])


ROWS = 128


def scores(place, queries_ref, own, swap_one, one, swap_two, two, out_ref, sum_ref, held):
    z, index, core = place[0], place[1], place[2]
    for tile in range(SUPER // ROWS):
        queries = queries_ref[tile * ROWS : (tile + 1) * ROWS]
        query_at = (
            ((tile // 2) ^ z) * HALF
            + (tile % 2) * ROWS
            + lax.broadcasted_iota(jnp.int32, (ROWS, SUPER), 0)
        )
        column = lax.broadcasted_iota(jnp.int32, (ROWS, SUPER), 1)
        highest = jnp.full((ROWS, 1), MASKED, F32)
        order = ((own, 0), (one, 2), (two, REACH), (swap_one, 1 + 2 * core), (swap_two, 3 - 2 * core))
        for slot, (piece, distance) in enumerate(order):
            source = z * 16 + index - distance
            part = nt(queries, piece[...]) * (512 ** (-0.5))
            if slot == 0:
                shift = z * HALF
                key_at = jnp.where(column < HALF, column + shift, column - shift)
                part = jnp.where(key_at <= query_at, part, MASKED)
            elif slot == 2:
                shift = jnp.where(source >= 16, HALF, 0)
                key_at = jnp.where(column < HALF, column + shift, column - shift)
                part = jnp.where((key_at > query_at) & (source >= 0), part, MASKED)
            else:
                part = jnp.where(source >= 0, part, MASKED)
            held[slot] = part
            highest = jnp.maximum(highest, jnp.max(part, axis=1, keepdims=True))
        total = jnp.zeros((ROWS, 1), F32)
        rows = slice(tile * ROWS, (tile + 1) * ROWS)
        for slot in range(5):
            weights = jnp.exp(held[slot] - highest)
            total = total + jnp.sum(weights, axis=1, keepdims=True)
            out_ref[slot, rows] = weights.astype(BF)
        sum_ref[rows] = jnp.broadcast_to(1.0 / total, (ROWS, 128))


def gathered(weights_ref, sum_ref, own, swap_one, one, swap_two, two, same_ref, other_ref):
    for half, out_ref in enumerate((same_ref, other_ref)):
        rows = slice(half * HALF, (half + 1) * HALF)
        result = jnp.zeros((HALF, 512), F32)
        for slot, piece in enumerate((own, one, two, swap_one, swap_two)):
            result = result + nn(weights_ref[slot, rows], piece[...])
        out_ref[...] = (result * sum_ref[rows, 0:1]).astype(BF)


def mix(place, near_ref, far_ref, normed_ref, w_ref, keep_ref, send_ref, *, block_num):
    z, core, pair = place[0], place[2], place[3]
    attended = jnp.where(z == block_num, near_ref[...], far_ref[...])
    combined = (attended.astype(F32) + normed_ref[...]).astype(BF)
    for step in range(2):
        for out_ref, whose in ((keep_ref, core), (send_ref, 1 - core)):
            column = pl.multiple_of(((pair ^ step) * 2 + whose) * 512, 512)
            out_ref[step] = nn(combined, w_ref[:, pl.ds(column, 512)]).astype(BF)


def mix_zero(*refs):
    mix(*refs, block_num=0)


def mix_one(*refs):
    mix(*refs, block_num=1)


def mixed_by(kernel, place, near, far, normed, w_out):
    return call(kernel, [smem()] + [vmem()] * 4, [((2, HALF, 512), BF)] * 2)(
        place, near, far, normed, w_out
    )


def ordered(values, *before):
    kept = lax.optimization_barrier((tuple(values), before))
    return list(kept[0])


def exchanged(pieces, axis):
    received = [pieces[0]]
    for step in range(1, len(pieces)):
        dx, dy, dz = (step if axis == name else 0 for name in "xyz")

        def route(x, y, z, zh, core):
            return (x ^ dx, y ^ dy, z ^ dz, zh, core)

        received.append(moved(pieces[step], route))
    return received


def shards(tokens, w_qkv, w_rate, w_out, fw_gain, fast_first, fast_third, fast_second):
    width = tokens.shape[2]
    ctx, head = lax.axis_index("ctx"), lax.axis_index("head")
    x, y, z = ctx // 8, (ctx // 2) % 4, ctx % 2
    zh, core = head // 2, head % 2
    index = 4 * x + (y & 2) + core
    place = jnp.stack([z, index, core, zh, x, y]).astype(jnp.int32)
    first, third, second = fast_first[0], fast_third[0], fast_second[0]

    natural, same, other = run_project(
        place, tokens, w_qkv.reshape(width, 1536)
    )
    same = moved(same, to_role_same)
    other = moved(other, to_role_other)
    grads = call(
        fast_grads,
        [smem()] + [vmem()] * 6,
        [((384, 512), BF)] * 4,
        scratch=(pltpu.VMEM((1536, 512), BF),),
        limit=24,
    )(place, tokens, w_rate.reshape(1, width), natural, first, third, second)
    same, other = ordered([same, other], *grads)
    grads = exchanged(grads, "x")
    queries, own_keys, own_values = (
        jnp.concatenate([half[at * HALF : (at + 1) * HALF] for half in (same, other)], axis=0)
        for at in range(3)
    )
    grads = call(
        reduce_x,
        [smem()] + [vmem()] * 4,
        [((96, 512), BF)] * 4,
        scratch=(pltpu.VMEM((384, 512), BF),),
    )(place, *grads)
    (own_keys,) = ordered([own_keys], grads[0])
    two_keys = moved(own_keys, quads_on(2))
    grads = ordered(exchanged(grads, "y"), own_values)
    (piece,) = call(reduce_y, [vmem()] * 4, [((96, 512), BF)])(*grads)
    (piece,) = call(reduce_z, [vmem()] * 2, [((96, 512), BF)])(*exchanged([piece] * 2, "z"))

    def onward(own, two):
        one = jnp.where(y >= 2, two, own)
        (two,) = ordered([two], one)
        return one, jnp.where(core == 0, own, two)

    (own_values,) = ordered([own_values], piece)
    two_values = moved(own_values, quads_on(2))
    (two_keys,) = ordered([two_keys], piece)
    one_keys, swap_two_keys = onward(own_keys, two_keys)
    piece = exchanged([piece] * 4, "y")
    piece = jnp.concatenate(ordered(piece, one_keys), axis=0)
    one_keys = moved(one_keys, across)
    swap_two_keys = moved(swap_two_keys, other_core)
    lines = [[8 * at_x + at for at_x in range(CTX_X)] for at in range(8)]
    sent = jnp.broadcast_to(piece[None], (CTX_X, 384, 512))
    parts = [lax.all_to_all(sent, "ctx", 0, 0, axis_index_groups=lines, tiled=True)]
    (two_values,) = ordered([two_values], sent)
    one_values, swap_two_values = onward(own_values, two_values)
    (queries,) = ordered([queries], piece)
    one_values = moved(one_values, across)
    swap_two_values = moved(swap_two_values, other_core)

    swap_one_keys = moved(one_keys, other_core)
    weights, sums = call(
        scores,
        [smem()] + [vmem()] * 6,
        [((5, SUPER, SUPER), BF), ((SUPER, 128), F32)],
        scratch=(pltpu.VMEM((5, ROWS, SUPER), F32),),
    )(place, queries, own_keys, swap_one_keys, one_keys, swap_two_keys, two_keys)
    parts = ordered(parts, weights)
    (held,) = call(
        update_start,
        [smem(), vmem()],
        [((3, 512, 512), BF)],
        scratch=(pltpu.VMEM((1536, 512), BF),),
        limit=24,
    )(place, *parts)
    (one_values,) = ordered([one_values], weights, held)
    swap_one_values = moved(one_values, other_core)
    near, far = call(gathered, [vmem()] * 7, [((HALF, 512), BF)] * 2)(
        weights, sums, own_values, swap_one_values, one_values, swap_two_values, two_values
    )
    (held,) = ordered([held], near, far)
    near = moved(near, to_role_same)
    far = moved(far, to_role_other)

    (normed_zero,) = call(
        fast_apply, [vmem()] * 5, [((HALF, 512), F32)]
    )(natural, first, third, second, fw_gain)
    (held,) = call(update_middle, [vmem()], [((3, 512, 512), BF)], limit=24)(held)
    normed_zero, near, far = ordered([normed_zero, near, far], held)
    keep, send = mixed_by(mix_zero, place, near, far, normed_zero, w_out[0])
    (held,) = ordered([held], send)
    taken = moved(send, other_core)
    new_first, new_third, new_second, normed_one = call(
        update_end,
        [vmem()] * 6,
        [((512, 512), F32)] * 3 + [((HALF, 512), F32)],
        scratch=(pltpu.VMEM((3, 512, 512), BF),),
        limit=24,
    )(held, first, third, second, natural, fw_gain)
    (taken,) = ordered([taken], normed_one)
    half_zero = keep.astype(F32) + taken.astype(F32)
    crossing = half_zero[1].astype(BF)
    (normed_one,) = ordered([normed_one], crossing)
    crossing = moved(crossing, other_pair)
    keep, send = mixed_by(mix_one, place, near, far, normed_one, w_out[0])
    half_one = keep.astype(F32) + moved(send, other_core).astype(F32)
    done_zero = half_zero[0] + crossing.astype(F32)
    done_one = half_one[0] + moved(half_one[1].astype(BF), other_pair).astype(F32)
    mixed = jnp.stack([done_zero, done_one]).astype(BF)
    return (mixed, new_first[None], new_third[None], new_second[None])


def solution(mesh):
    placed = (
        P(None, "ctx", None),
        P(None, "head", None),
        P(None, "head"),
        P("head", None, None),
        P("head", None),
        P("head", None, None),
        P("head", None, None),
        P("head", None, None),
    )
    return jax.shard_map(
        shards,
        mesh=mesh,
        in_specs=placed,
        out_specs=(
            P(None, "ctx", "head"),
            P("head", None, None),
            P("head", None, None),
            P("head", None, None),
        ),
        check_vma=False,
    )
```

```python
import jax
import jax.numpy as jnp
from jax import lax
from jax.experimental import pallas as pl
from jax.experimental.pallas import tpu as pltpu
from jax.sharding import PartitionSpec as P

NS_STEPS = 5
FIRST_STEPS = 1
MIDDLE_STEPS = 2
HALF = 256
SUPER = 512
REACH = 4
BF = jnp.bfloat16
F32 = jnp.float32

coeff_a = 3.4445
coeff_b = -4.775
coeff_c = 2.0315
fast_step = 0.5
norm_eps = 1e-06
MASKED = -1e30

CTX_X, CTX_Y, CTX_Z = 4, 4, 2


def nn(left, right):
    return lax.dot_general(left, right, (((1,), (0,)), ((), ())), preferred_element_type=F32)


def nt(left, right):
    return lax.dot_general(left, right, (((1,), (1,)), ((), ())), preferred_element_type=F32)


def tn(left, right):
    return lax.dot_general(left, right, (((0,), (0,)), ((), ())), preferred_element_type=F32)


def moved(value, route):
    pairs = []
    for ctx in range(CTX_X * CTX_Y * CTX_Z):
        x, y, z = ctx // 8, (ctx // 2) % 4, ctx % 2
        for head in range(4):
            target = route(x, y, z, head // 2, head % 2)
            if target is not None:
                tx, ty, tz, th, tc = target
                pairs.append((ctx * 4 + head, (tx * 8 + ty * 2 + tz) * 4 + th * 2 + tc))
    return lax.ppermute(value, ("ctx", "head"), pairs)


def to_role_same(x, y, z, zh, core):
    return (x, (y & 2) + core, z, zh, y & 1)


def to_role_other(x, y, z, zh, core):
    return (x, (y & 2) + core, 1 - z, zh, y & 1)


def quads_on(steps):
    def route(x, y, z, zh, core):
        place = z * 8 + 2 * x + (y >> 1) + steps
        if place >= 16:
            return None
        quad = place % 8
        return (quad // 2, (quad % 2) * 2 + (y & 1), place // 8, zh, core)

    return route


def across(x, y, z, zh, core):
    return (x, y ^ 2, z, zh, core)


def other_core(x, y, z, zh, core):
    return (x, y, z, zh, 1 - core)


def other_pair(x, y, z, zh, core):
    return (x, y, z, 1 - zh, core)


def vmem():
    return pl.BlockSpec(memory_space=pltpu.VMEM)


def smem():
    return pl.BlockSpec(memory_space=pltpu.SMEM)


def call(kernel, specs, outs, flops=1 << 20, scratch=(), limit=16):
    return pl.pallas_call(
        kernel,
        in_specs=specs,
        out_specs=[vmem()] * len(outs),
        out_shape=[jax.ShapeDtypeStruct(shape, dtype) for shape, dtype in outs],
        scratch_shapes=list(scratch),
        compiler_params=pltpu.CompilerParams(vmem_limit_bytes=limit << 20),
        cost_estimate=pl.CostEstimate(flops=flops, bytes_accessed=1 << 10, transcendentals=0),
        name=kernel.__name__,
    )


CHUNKS = 4
DEPTH = 512


def project(place, tokens_ref, w_ref, natural_ref, same, other, tokens_held, held, total, sems):
    copies = []
    for j in range(CHUNKS):
        rows = pl.ds(j * DEPTH, DEPTH)
        copies.append(
            (
                pltpu.make_async_copy(
                    tokens_ref.at[:, :, rows], tokens_held.at[:, :, rows], sems.at[CHUNKS + j]
                ),
                pltpu.make_async_copy(w_ref.at[rows], held.at[rows], sems.at[j]),
            )
        )
    for pair in copies:
        for copy in pair:
            copy.start()
    z = place[0]
    for j, pair in enumerate(copies):
        for copy in pair:
            copy.wait()
        depth = slice(j * DEPTH, (j + 1) * DEPTH)
        tokens = tokens_held[:, :, depth].reshape(2 * HALF, DEPTH)
        for at in range(3):
            columns = slice(at * 512, (at + 1) * 512)
            part = nn(tokens, held[depth, columns])
            if j == 0:
                total[:, columns] = part
            elif j < CHUNKS - 1:
                total[:, columns] += part
            else:
                result = (total[:, columns] + part).astype(BF)
                low, high = result[:HALF], result[HALF:]
                natural_ref[0, :, columns] = low
                natural_ref[1, :, columns] = high
                rows = slice(at * HALF, (at + 1) * HALF)
                same[rows] = jnp.where(z == 0, low, high)
                other[rows] = jnp.where(z == 0, high, low)


def run_project(place, tokens, weights):
    return call(
        project,
        [smem()] + [pl.BlockSpec(memory_space=pltpu.HBM)] * 2,
        [((2, HALF, 1536), BF)] + [((3 * HALF, 512), BF)] * 2,
        scratch=(
            pltpu.VMEM((2, HALF, 2048), BF),
            pltpu.VMEM((2048, 1536), BF),
            pltpu.VMEM((SUPER, 1536), F32),
            pltpu.SemaphoreType.DMA((2 * CHUNKS,)),
        ),
        limit=50,
    )(place, tokens, weights)


def spread(whole, outs, at):
    rows = outs[0].shape[0]
    for step, ref in enumerate(outs):
        start = pl.multiple_of((at ^ step) * rows, rows)
        ref[...] = whole[pl.ds(start, rows)]


def fast_grads(place, tokens_ref, rate_ref, qkv_ref, first_ref, third_ref, second_ref, *rest):
    out_ref = rest[4]
    drive = jnp.sum(
        tokens_ref[0].astype(F32) * rate_ref[...].astype(F32), axis=1, keepdims=True
    )
    rates = jnp.maximum(drive, 0.0) + jnp.log1p(jnp.exp(-jnp.abs(drive)))
    keys = qkv_ref[0, :, 512:1024]
    values = qkv_ref[0, :, 1024:]
    hidden_one = nn(keys, first_ref[...].astype(BF))
    hidden_three = nn(keys, third_ref[...].astype(BF))
    target = (-rates * values.astype(F32)).astype(BF)
    dactiv = nt(target, second_ref[...].astype(BF))
    sigma = jax.nn.sigmoid(hidden_one)
    silu = hidden_one * sigma
    activ = (silu * hidden_three).astype(BF)
    d_first = (dactiv * hidden_three * (sigma * (1.0 + hidden_one * (1.0 - sigma)))).astype(BF)
    d_third = (dactiv * silu).astype(BF)
    out_ref[0:512] = tn(keys, d_first).astype(BF)
    out_ref[512:1024] = tn(keys, d_third).astype(BF)
    out_ref[1024:1536] = tn(activ, target).astype(BF)
    spread(out_ref, rest[:4], place[4])


def summed(refs):
    total = refs[0][...].astype(F32)
    for ref in refs[1:]:
        total = total + ref[...].astype(F32)
    return total.astype(BF)


def reduce_x(place, *refs):
    refs[8][...] = summed(refs[:4])
    spread(refs[8], refs[4:8], place[5])


def reduce_y(*refs):
    refs[4][...] = summed(refs[:4])


def reduce_z(*refs):
    refs[2][...] = summed(refs[:2])


def applied(queries, first, third, second, gain):
    hidden_one = nn(queries, first)
    hidden_three = nn(queries, third)
    activ = (jax.nn.silu(hidden_one) * hidden_three).astype(BF)
    fast_out = nn(activ, second)
    mean = jnp.mean(fast_out * fast_out, axis=1, keepdims=True)
    return fast_out * lax.rsqrt(mean + norm_eps) * gain


def fast_apply(qkv_ref, first_ref, third_ref, second_ref, gain_ref, out_ref):
    out_ref[...] = applied(
        qkv_ref[0, :, :512],
        first_ref[...].astype(BF),
        third_ref[...].astype(BF),
        second_ref[...].astype(BF),
        gain_ref[...],
    )


def advanced(now):
    grams = [nt(x, x) for x in now]
    narrow = [gram.astype(BF) for gram in grams]
    polys = [
        (coeff_b * gram + coeff_c * nn(low, low)).astype(BF)
        for gram, low in zip(grams, narrow)
    ]
    return [coeff_a * x.astype(F32) + nn(poly, x) for x, poly in zip(now, polys)]


def repeated(ref, steps):
    @pl.loop(0, steps)
    def _(step):
        for which, value in enumerate(advanced([ref[which] for which in range(3)])):
            ref[which] = value.astype(BF)


def update_start(place, parts_ref, out_ref, grad_ref):
    y = place[5]
    for at_x in range(4):
        for across_y in range(4):
            start = at_x * 384 + (y ^ across_y) * 96
            at = across_y * 96
            grad_ref[pl.ds(pl.multiple_of(start, 96), 96)] = parts_ref[
                at_x, at : at + 96
            ]
    for which in range(3):
        grad = grad_ref[which * 512 : (which + 1) * 512].astype(F32)
        scale = lax.rsqrt(jnp.sum(grad * grad, keepdims=True) + norm_eps)
        out_ref[which] = (grad * scale).astype(BF)
    repeated(out_ref, FIRST_STEPS)


def update_middle(in_ref, out_ref):
    out_ref[...] = in_ref[...]
    repeated(out_ref, MIDDLE_STEPS)


def update_end(
    in_ref,
    first_ref,
    third_ref,
    second_ref,
    qkv_ref,
    gain_ref,
    new_first_ref,
    new_third_ref,
    new_second_ref,
    normed_ref,
    held,
):
    held[...] = in_ref[...]
    repeated(held, NS_STEPS - 1 - FIRST_STEPS - MIDDLE_STEPS)
    last = advanced([held[which] for which in range(3)])
    old = (first_ref, third_ref, second_ref)
    new = [ref[...] - fast_step * value for ref, value in zip(old, last)]
    for ref, value in zip((new_first_ref, new_third_ref, new_second_ref), new):
        ref[...] = value
    narrow = [weight.astype(BF) for weight in new]
    normed_ref[...] = applied(qkv_ref[1, :, :512], *narrow, gain_ref[...])


ROWS = 128


def scores(place, queries_ref, own, swap_one, one, swap_two, two, out_ref, sum_ref, held):
    z, index, core = place[0], place[1], place[2]
    for tile in range(SUPER // ROWS):
        queries = queries_ref[tile * ROWS : (tile + 1) * ROWS]
        query_at = (
            ((tile // 2) ^ z) * HALF
            + (tile % 2) * ROWS
            + lax.broadcasted_iota(jnp.int32, (ROWS, SUPER), 0)
        )
        column = lax.broadcasted_iota(jnp.int32, (ROWS, SUPER), 1)
        highest = jnp.full((ROWS, 1), MASKED, F32)
        order = ((own, 0), (one, 2), (two, REACH), (swap_one, 1 + 2 * core), (swap_two, 3 - 2 * core))
        for slot, (piece, distance) in enumerate(order):
            source = z * 16 + index - distance
            part = nt(queries, piece[...]) * (512 ** (-0.5))
            if slot == 0:
                shift = z * HALF
                key_at = jnp.where(column < HALF, column + shift, column - shift)
                part = jnp.where(key_at <= query_at, part, MASKED)
            elif slot == 2:
                shift = jnp.where(source >= 16, HALF, 0)
                key_at = jnp.where(column < HALF, column + shift, column - shift)
                part = jnp.where((key_at > query_at) & (source >= 0), part, MASKED)
            else:
                part = jnp.where(source >= 0, part, MASKED)
            held[slot] = part
            highest = jnp.maximum(highest, jnp.max(part, axis=1, keepdims=True))
        total = jnp.zeros((ROWS, 1), F32)
        rows = slice(tile * ROWS, (tile + 1) * ROWS)
        for slot in range(5):
            weights = jnp.exp(held[slot] - highest)
            total = total + jnp.sum(weights, axis=1, keepdims=True)
            out_ref[slot, rows] = weights.astype(BF)
        sum_ref[rows] = jnp.broadcast_to(1.0 / total, (ROWS, 128))


def gathered(weights_ref, sum_ref, own, swap_one, one, swap_two, two, same_ref, other_ref):
    for half, out_ref in enumerate((same_ref, other_ref)):
        rows = slice(half * HALF, (half + 1) * HALF)
        result = jnp.zeros((HALF, 512), F32)
        for slot, piece in enumerate((own, one, two, swap_one, swap_two)):
            result = result + nn(weights_ref[slot, rows], piece[...])
        out_ref[...] = (result * sum_ref[rows, 0:1]).astype(BF)


def mix(place, near_ref, far_ref, normed_ref, w_ref, keep_ref, send_ref, *, block_num):
    z, core, pair = place[0], place[2], place[3]
    attended = jnp.where(z == block_num, near_ref[...], far_ref[...])
    combined = (attended.astype(F32) + normed_ref[...]).astype(BF)
    for step in range(2):
        for out_ref, whose in ((keep_ref, core), (send_ref, 1 - core)):
            column = pl.multiple_of(((pair ^ step) * 2 + whose) * 512, 512)
            out_ref[step] = nn(combined, w_ref[:, pl.ds(column, 512)]).astype(BF)


def mix_zero(*refs):
    mix(*refs, block_num=0)


def mix_one(*refs):
    mix(*refs, block_num=1)


def mixed_by(kernel, place, near, far, normed, w_out):
    return call(kernel, [smem()] + [vmem()] * 4, [((2, HALF, 512), BF)] * 2)(
        place, near, far, normed, w_out
    )


def ordered(values, *before):
    kept = lax.optimization_barrier((tuple(values), before))
    return list(kept[0])


def exchanged(pieces, axis):
    received = [pieces[0]]
    for step in range(1, len(pieces)):
        dx, dy, dz = (step if axis == name else 0 for name in "xyz")

        def route(x, y, z, zh, core):
            return (x ^ dx, y ^ dy, z ^ dz, zh, core)

        received.append(moved(pieces[step], route))
    return received


def shards(tokens, w_qkv, w_rate, w_out, fw_gain, fast_first, fast_third, fast_second):
    width = tokens.shape[2]
    ctx, head = lax.axis_index("ctx"), lax.axis_index("head")
    x, y, z = ctx // 8, (ctx // 2) % 4, ctx % 2
    zh, core = head // 2, head % 2
    index = 4 * x + (y & 2) + core
    place = jnp.stack([z, index, core, zh, x, y]).astype(jnp.int32)
    first, third, second = fast_first[0], fast_third[0], fast_second[0]

    natural, same, other = run_project(
        place, tokens, w_qkv.reshape(width, 1536)
    )
    same = moved(same, to_role_same)
    other = moved(other, to_role_other)
    grads = call(
        fast_grads,
        [smem()] + [vmem()] * 6,
        [((384, 512), BF)] * 4,
        scratch=(pltpu.VMEM((1536, 512), BF),),
        limit=24,
    )(place, tokens, w_rate.reshape(1, width), natural, first, third, second)
    same, other = ordered([same, other], *grads)
    grads = exchanged(grads, "x")
    queries, own_keys, own_values = (
        jnp.concatenate([half[at * HALF : (at + 1) * HALF] for half in (same, other)], axis=0)
        for at in range(3)
    )
    grads = call(
        reduce_x,
        [smem()] + [vmem()] * 4,
        [((96, 512), BF)] * 4,
        scratch=(pltpu.VMEM((384, 512), BF),),
    )(place, *grads)
    (own_keys,) = ordered([own_keys], grads[0])
    two_keys = moved(own_keys, quads_on(2))
    grads = ordered(exchanged(grads, "y"), own_values)
    (piece,) = call(reduce_y, [vmem()] * 4, [((96, 512), BF)])(*grads)
    (piece,) = call(reduce_z, [vmem()] * 2, [((96, 512), BF)])(*exchanged([piece] * 2, "z"))

    def onward(own, two):
        one = jnp.where(y >= 2, two, own)
        (two,) = ordered([two], one)
        return one, jnp.where(core == 0, own, two)

    (own_values,) = ordered([own_values], piece)
    two_values = moved(own_values, quads_on(2))
    (two_keys,) = ordered([two_keys], piece)
    one_keys, swap_two_keys = onward(own_keys, two_keys)
    piece = exchanged([piece] * 4, "y")
    piece = jnp.concatenate(ordered(piece, one_keys), axis=0)
    one_keys = moved(one_keys, across)
    swap_two_keys = moved(swap_two_keys, other_core)
    lines = [[8 * at_x + at for at_x in range(CTX_X)] for at in range(8)]
    sent = jnp.broadcast_to(piece[None], (CTX_X, 384, 512))
    parts = [lax.all_to_all(sent, "ctx", 0, 0, axis_index_groups=lines, tiled=True)]
    (two_values,) = ordered([two_values], sent)
    one_values, swap_two_values = onward(own_values, two_values)
    (normed_zero,) = call(
        fast_apply, [vmem()] * 5, [((HALF, 512), F32)]
    )(natural, first, third, second, fw_gain)
    (queries,) = ordered([queries], piece, normed_zero)
    one_values = moved(one_values, across)
    swap_two_values = moved(swap_two_values, other_core)

    swap_one_keys = moved(one_keys, other_core)
    weights, sums = call(
        scores,
        [smem()] + [vmem()] * 6,
        [((5, SUPER, SUPER), BF), ((SUPER, 128), F32)],
        scratch=(pltpu.VMEM((5, ROWS, SUPER), F32),),
    )(place, queries, own_keys, swap_one_keys, one_keys, swap_two_keys, two_keys)
    parts = ordered(parts, weights)
    (held,) = call(
        update_start,
        [smem(), vmem()],
        [((3, 512, 512), BF)],
        scratch=(pltpu.VMEM((1536, 512), BF),),
        limit=24,
    )(place, *parts)
    (one_values,) = ordered([one_values], weights, held)
    swap_one_values = moved(one_values, other_core)
    near, far = call(gathered, [vmem()] * 7, [((HALF, 512), BF)] * 2)(
        weights, sums, own_values, swap_one_values, one_values, swap_two_values, two_values
    )
    (held,) = ordered([held], near, far)
    near = moved(near, to_role_same)
    far = moved(far, to_role_other)

    (held,) = call(update_middle, [vmem()], [((3, 512, 512), BF)], limit=24)(held)
    normed_zero, near, far = ordered([normed_zero, near, far], held)
    keep, send = mixed_by(mix_zero, place, near, far, normed_zero, w_out[0])
    (held,) = ordered([held], send)
    taken = moved(send, other_core)
    new_first, new_third, new_second, normed_one = call(
        update_end,
        [vmem()] * 6,
        [((512, 512), F32)] * 3 + [((HALF, 512), F32)],
        scratch=(pltpu.VMEM((3, 512, 512), BF),),
        limit=24,
    )(held, first, third, second, natural, fw_gain)
    (taken,) = ordered([taken], normed_one)
    half_zero = keep.astype(F32) + taken.astype(F32)
    crossing = half_zero[1].astype(BF)
    (normed_one,) = ordered([normed_one], crossing)
    crossing = moved(crossing, other_pair)
    keep, send = mixed_by(mix_one, place, near, far, normed_one, w_out[0])
    half_one = keep.astype(F32) + moved(send, other_core).astype(F32)
    done_zero = half_zero[0] + crossing.astype(F32)
    done_one = half_one[0] + moved(half_one[1].astype(BF), other_pair).astype(F32)
    mixed = jnp.stack([done_zero, done_one]).astype(BF)
    return (mixed, new_first[None], new_third[None], new_second[None])


def solution(mesh):
    placed = (
        P(None, "ctx", None),
        P(None, "head", None),
        P(None, "head"),
        P("head", None, None),
        P("head", None),
        P("head", None, None),
        P("head", None, None),
        P("head", None, None),
    )
    return jax.shard_map(
        shards,
        mesh=mesh,
        in_specs=placed,
        out_specs=(
            P(None, "ctx", "head"),
            P("head", None, None),
            P("head", None, None),
            P("head", None, None),
        ),
        check_vma=False,
    )
```
